128 devices in a mesh: pose: 32 (over z, y, core), dom: 4 (over x).
Axes of the slice: x: 4, y: 4, z: 4, core: 2. Of those that a mesh axis runs over, the one named last changes fastest.
Arguments:
- particles: bfloat16 [16384, 4096], P(('pose', 'dom')), may hold values from -16 to 16
- candidates: int32 [16384, 2], P(('pose', 'dom')), may hold values from 0 to 63, all different within a row; in each aligned block of 128 rows (0 to 127, 128 to 255, ...) at most 12 rows name the same one
- ctf_ids: int32 [16384], P(('pose', 'dom')), may hold values from 0 to 15
- offsets: int32 [16384, 2, 9], P(('pose', 'dom')), may hold values from -3 to 3
- ctf_table: float32 [16, 2048], replicated, may hold values from -1 to 1
- sigma_sq: float32 [2048], replicated, may hold values from 0.5 to 2
- projections: bfloat16 [64, 256, 4096], P('pose', 'dom'), may hold values from -6 to 6
Outputs:
- class_prob: float32 [16384, 2], P(('pose', 'dom'))
- mean_shift: float32 [16384, 2], P(('pose', 'dom'))
The draws below stay inside these ranges and needn't reach their ends.
Inputs may be any that keep to these rules, and one draw needn't show every extreme that they name: `candidates`: each particle names 2 different classes; among the rows of one device no class is named by more than 12 rows, and on some device one class is named by exactly 12.
All inputs are finite; a program needn't handle non-finite values.
Results may differ from the reference program's by a relative error of at most 0.0025.
The reference program's roundings to bfloat16 on the way (of `shifted`) count: a program that leaves them out, or rounds other values in their place, can miss the bound.
Values may be sent and summed in bfloat16 or wider, within the bound.
A program may use at most 192 MiB of HBM per device.

```python
import math
import jax
import jax.numpy as jnp
import numpy as np
from jax import lax

P_SIZE = 2048
ORI = 256
TRANS = 9
TOP = 2
NCTF = 16
BOX = 128
PART_DEV = 128
CLASSES = 64
NPART = 16384
MOST = 12


def draw_particles(key, part):
    base_key = jax.random.fold_in(key, 21)
    values = jnp.clip(jax.random.normal(base_key, (NPART, 2 * P_SIZE), jnp.float32), -6.0, 6.0)
    return jnp.clip(values, -16.0, 16.0).astype(jnp.bfloat16)


def draw_projections(key, part):
    noise = jnp.clip(jax.random.normal(jax.random.fold_in(key, 31), (CLASSES, ORI, 2 * P_SIZE), jnp.float32), -6.0, 6.0)
    values = noise
    return jnp.clip(values, -6.0, 6.0).astype(jnp.bfloat16)


def draw_ctf_table(key, part):
    values = jax.random.uniform(jax.random.fold_in(key, 41), (NCTF, P_SIZE), jnp.float32, -1.0, 1.0)
    return values


def with_ends(array, rng, smallest, largest):
    longest = array.shape.index(max(array.shape))
    spots = []
    for shift in (0, 1):
        where = [jax.random.randint(jax.random.fold_in(rng, axis), (), 0, length) for axis, length in enumerate(array.shape)]
        where[longest] = (where[longest] + shift) % array.shape[longest]
        spots.append(tuple(where))
    return array.at[spots[0]].set(smallest).at[spots[1]].set(largest)


def assign_block(rng, own, number, rows, count, top, reach, skew):
    sequence = jax.random.permutation(rng, count)
    heavy_load, common = portions_of(count, rows * top, reach, skew, True), portions_of(count, rows * top, reach, skew, False)
    places = jnp.arange(count)

    def named(tallies, rotation):
        used = int((tallies > 0).sum())
        fixed = max(1, used // 4)
        moved = fixed + (places - fixed + rotation * (used - fixed)) % max(1, count - fixed)
        return jnp.zeros((count,), jnp.int32).at[sequence[jnp.where(places < fixed, places, moved)]].set(jnp.asarray(tallies, jnp.int32))

    tallies = jnp.where(number % 4 == 0, named(heavy_load, number // 4), named(common, number - number // 4 - 1))
    mixed = jax.random.permutation(jax.random.fold_in(own, 3), count)
    donor, receiver = mixed[0:count // 2 * 2:2], mixed[1:count // 2 * 2:2]
    slack = jnp.minimum(tallies[donor] - 1, reach - tallies[receiver]) // 2
    slack = jnp.where((donor == sequence[0]) | (receiver == sequence[0]) | (tallies[receiver] == 0), 0, jnp.maximum(slack, 0))
    moved = jax.random.randint(jax.random.fold_in(own, 4), (count // 2,), 0, 1 << 20) % (slack + 1)
    tallies = tallies.at[donor].add(-moved).at[receiver].add(moved)
    items = jnp.searchsorted(jnp.cumsum(tallies), jnp.arange(rows * top), side="right").astype(jnp.int32)
    table = items.reshape(top, rows).T
    table = table[jax.random.permutation(jax.random.fold_in(own, 1), rows)]
    rotation = jax.random.randint(jax.random.fold_in(own, 2), (rows, 1), 0, top)
    return jnp.take_along_axis(table, (jnp.arange(top)[None, :] + rotation) % top, axis=1)


def portions_of(number_of, total, limit, skew, full):
    loads = [(1 << 20) // math.isqrt(grade ** skew) + 1 for grade in range(1, number_of + 1)]
    largest = limit if full else min(limit, max(-(-total // number_of), total * loads[0] // sum(loads)))
    least = 1 if total - largest >= number_of - 1 else 0
    holding, surplus = [largest] + [least] * (number_of - 1), total - largest - least * (number_of - 1)
    while surplus > 0:
        free = [i for i in range(1, number_of) if holding[i] < largest] or [i for i in range(1, number_of) if holding[i] < limit]
        pool, budget = sum([loads[i] for i in free]), surplus
        for i in free:
            addition = min(limit - holding[i], max(1, budget * loads[i] // pool), surplus)
            holding[i] = holding[i] + addition
            surplus = surplus - addition
    return np.array(holding)


def setup_inputs(seed: int = 0) -> dict:
    seeds = jax.random.split(jax.random.key(seed), 8)
    particles = draw_particles(jax.random.fold_in(seeds[7], 71), 0)
    candidates_keys = jax.random.split(jax.random.fold_in(seeds[1], 1), NPART // PART_DEV)
    candidates_turns = jax.random.permutation(jax.random.fold_in(seeds[1], 3), NPART // PART_DEV)
    candidates = jax.vmap(lambda own, number: assign_block(jax.random.fold_in(seeds[1], 2), own, number, PART_DEV, CLASSES, TOP, MOST, 2))(candidates_keys, candidates_turns).reshape((NPART, TOP))
    ctf_ids = with_ends(jax.random.randint(seeds[2], (NPART,), 0, NCTF), jax.random.fold_in(seeds[2], 1), 0, NCTF - 1).astype(jnp.int32)
    offsets = with_ends(jax.random.randint(seeds[3], (NPART, 2, TRANS), -3, 4), jax.random.fold_in(seeds[3], 1), -3, 3).astype(jnp.int32)
    ctf_table = draw_ctf_table(jax.random.fold_in(seeds[7], 71), 0)
    sigma_sq = jnp.clip(jnp.exp(jax.random.uniform(seeds[5], (P_SIZE,), jnp.float32, math.log(0.5), math.log(2.0))), 0.5, 2.0)
    projections = draw_projections(jax.random.fold_in(seeds[7], 71), 0)
    return {"particles": particles, "candidates": candidates, "ctf_ids": ctf_ids, "offsets": offsets, "ctf_table": ctf_table, "sigma_sq": sigma_sq, "projections": projections}


two_pi = 6.283185307179586


def reference(particles, candidates, ctf_ids, offsets, ctf_table, sigma_sq, projections):
    stacked = projections.astype(jnp.float32)
    power_rows = stacked[:, :, :P_SIZE] ** 2 + stacked[:, :, P_SIZE:] ** 2
    pixel_index = jnp.arange(P_SIZE, dtype=jnp.int32)
    freq_x = ((pixel_index % 64) - 32).astype(jnp.float32) * (two_pi / BOX)
    freq_y = (pixel_index // 64).astype(jnp.float32) * (two_pi / BOX)
    block_rows = 32

    def one_block(block_index):
        first_row = (block_index * block_rows).astype(jnp.int32)
        particle_rows = lax.dynamic_slice_in_dim(particles, first_row, block_rows, 0).astype(jnp.float32)
        chosen = lax.dynamic_slice_in_dim(candidates, first_row, block_rows, 0)
        shifts = lax.dynamic_slice_in_dim(offsets, first_row, block_rows, 0).astype(jnp.float32)
        ctf_index = lax.dynamic_slice_in_dim(ctf_ids, first_row, block_rows, 0)
        ctf_rows = ctf_table[ctf_index]
        weight = ctf_rows / sigma_sq[None, :]
        damping = weight * ctf_rows
        phase_angle = shifts[:, 0, :, None] * freq_x + shifts[:, 1, :, None] * freq_y
        cosine = jnp.cos(phase_angle)
        sine_part = jnp.sin(phase_angle)
        real_part = particle_rows[:, None, :P_SIZE]
        imag_part = particle_rows[:, None, P_SIZE:]
        shifted = jnp.concatenate([weight[:, None, :] * (real_part * cosine + imag_part * sine_part),
                                   weight[:, None, :] * (imag_part * cosine - real_part * sine_part)], axis=2)
        shifted = lax.optimization_barrier(shifted.astype(jnp.bfloat16)).astype(jnp.float32)
        weights_log = []
        totals = []
        moments_x = []
        moments_y = []
        for column in range(TOP):
            class_col = chosen[:, column]
            class_views = stacked[class_col]
            class_power = power_rows[class_col]
            scores = jnp.einsum('btk,bok->bto', shifted, class_views, precision=lax.Precision.HIGHEST)
            penalty = -0.5 * jnp.einsum('bp,bop->bo', damping, class_power, precision=lax.Precision.HIGHEST)
            scores = scores + penalty[:, None, :]
            highest = jnp.max(scores, axis=(1, 2))
            exp_terms = jnp.exp(scores - highest[:, None, None])
            per_shift = jnp.sum(exp_terms, axis=2)
            total = jnp.sum(per_shift, axis=1)
            weights_log.append(highest + jnp.log(total))
            totals.append(total)
            moments_x.append(jnp.sum(per_shift * shifts[:, 0, :], axis=1))
            moments_y.append(jnp.sum(per_shift * shifts[:, 1, :], axis=1))
        log_weight = jnp.stack(weights_log, axis=1)
        total_all = jnp.stack(totals, axis=1)
        highest_log = jnp.max(log_weight, axis=1, keepdims=True)
        raw_weight = jnp.exp(log_weight - highest_log)
        class_prob = raw_weight / jnp.sum(raw_weight, axis=1, keepdims=True)
        mean_x = jnp.sum(class_prob * jnp.stack(moments_x, axis=1) / total_all, axis=1)
        mean_y = jnp.sum(class_prob * jnp.stack(moments_y, axis=1) / total_all, axis=1)
        return class_prob, jnp.stack([mean_x, mean_y], axis=1)

    prob_blocks, mean_blocks = lax.map(one_block, jnp.arange(NPART // block_rows, dtype=jnp.int32))
    return prob_blocks.reshape(NPART, TOP), mean_blocks.reshape(NPART, 2)
```

```python
import math

import jax
import jax.numpy as jnp
import numpy as np
from jax import lax
from jax.experimental import pallas as pl
from jax.experimental.pallas import tpu as pltpu
from jax.sharding import PartitionSpec as P

MESH = pl.DeviceIdType.MESH
BOX = 128
PIX = 2048
TRANS = 9
CAP = 12
PEERS = 32
CHUNK = 512
WIDE = 6400
ROWS = 864


def trig_table():
    pixel = np.arange(PIX)
    kx, ky = pixel % 64 - 32, pixel // 64
    both = np.zeros((49, 2 * PIX), np.float64)
    for ox in range(-3, 4):
        for oy in range(-3, 4):
            angle = 2.0 * math.pi * ((kx * ox + ky * oy) % BOX) / BOX
            both[(ox + 3) * 7 + oy + 3] = np.concatenate([np.cos(angle), np.sin(angle)])
    table = np.zeros((256, 2 * PIX), jnp.bfloat16)
    left = both
    for part in range(3):
        piece = left.astype(jnp.bfloat16)
        table[64 * part : 64 * part + 49] = piece
        left = left - piece.astype(np.float64)
    return table


def unpack_perm():
    perm = np.zeros((2, 96, 128), np.float32)
    for m in range(48):
        src, k = divmod(m, CAP)
        perm[:, m, src * 16 + k] = 1.0
        for part in range(2):
            col = src * 16 + 12 + k if k < 4 else 64 + src * 16 + 8 * part + k - 4
            perm[part, 48 + m, col] = 1.0
    return perm.astype(jnp.bfloat16)


def dot(a, b):
    return jnp.dot(a, b, preferred_element_type=jnp.float32)


def dot_nt(a, b):
    return lax.dot_general(a, b, (((1,), (1,)), ((), ())), preferred_element_type=jnp.float32)


def split3(value):
    first = value.astype(jnp.bfloat16)
    rest = value - first.astype(jnp.float32)
    second = rest.astype(jnp.bfloat16)
    third = (rest - second.astype(jnp.float32)).astype(jnp.bfloat16)
    return first, second, third


def flag(cond):
    return jnp.where(cond, 1.0, 0.0).astype(jnp.bfloat16)


def fiota(shape, dim):
    return lax.broadcasted_iota(jnp.int32, shape, dim).astype(jnp.float32)


def kernel(
    x_ref,
    meta_ref,
    candt_ref,
    cand_ref,
    ctf_ref,
    sig_ref,
    perm_ref,
    trig_hbm,
    proj_hbm,
    prob_ref,
    mean_ref,
    send,
    recv,
    pbuf,
    trig,
    q_s,
    s1,
    s2,
    wtab,
    pentab,
    oh_s,
    cos_s,
    sin_s,
    a_re,
    a_im,
    acc,
    stat_out,
    stat_in,
    send_sem,
    recv_sem,
    back_send,
    back_recv,
    ag_send,
    ag_recv,
    local_sem,
):
    me = lax.axis_index("pose")
    dom = lax.axis_index("dom")
    core, my, mz = lax.rem(me, 2), lax.rem(me // 2, 4), me // 8

    def flip(a, b):
        hi = lax.rem(a // 2 + b // 2, 2)
        lo = lax.rem(lax.rem(a, 2) + lax.rem(b, 2), 2)
        return 2 * hi + lo

    def partner(j):
        dy = lax.rem(j // 2, 4)
        dz = lax.rem(dy + j // 8, 4)
        return flip(mz, dz) * 8 + flip(my, dy) * 2 + lax.rem(core + lax.rem(j, 2), 2)

    def at(p):
        return {"pose": p, "dom": dom}

    right = {"pose": me, "dom": lax.rem(dom + 1, 4)}
    left = {"pose": me, "dom": lax.rem(dom + 3, 4)}
    across = {"pose": me, "dom": lax.rem(dom + 2, 4)}

    barrier = pltpu.get_barrier_semaphore()

    def greet(j, carry):
        pl.semaphore_signal(barrier, inc=1, device_id=at(partner(j)), device_id_type=MESH)
        return carry

    lax.fori_loop(1, PEERS, greet, 0)
    for other in (right, left, across):
        pl.semaphore_signal(barrier, inc=1, device_id=other, device_id_type=MESH)

    own_copies = [
        pltpu.make_async_copy(proj_hbm.at[c], pbuf.at[c, pl.ds(0, 64)], local_sem.at[c])
        for c in range(2)
    ]
    own_copies.append(pltpu.make_async_copy(trig_hbm, trig, local_sem.at[2]))
    for copy in own_copies:
        copy.start()

    class_rows = lax.broadcasted_iota(jnp.int32, (64, 128), 0)
    named = (class_rows == candt_ref[0:1, :]) | (class_rows == candt_ref[1:2, :])
    before = flag(
        lax.broadcasted_iota(jnp.int32, (128, 128), 0)
        < lax.broadcasted_iota(jnp.int32, (128, 128), 1)
    )
    q_s[...] = jnp.where(named, dot(flag(named), before), -1.0)
    slot_rows = fiota((16, 128), 0)

    def choose(j, carry):
        p = partner(j)
        qa = q_s[pl.ds(2 * p, 1), :]
        qb = q_s[pl.ds(2 * p + 1, 1), :]
        rows = pl.ds(pl.multiple_of(16 * j, 16), 16)
        s1[rows, :] = flag(jnp.where(slot_rows < 12.0, qa, qb) == jnp.where(slot_rows < 12.0, slot_rows, slot_rows - 12.0))
        s2[rows, 0:128] = flag((qb == slot_rows + 4.0) & (slot_rows < 8.0))
        s2[rows, 128:256] = flag((qb == slot_rows - 4.0) & (slot_rows >= 8.0))
        return carry

    lax.fori_loop(0, PEERS, choose, 0)

    def block(ref, j):
        return ref.at[pl.ds(pl.multiple_of(16 * j, 16), 16), :]

    def row_copy(j):
        return pltpu.make_async_remote_copy(
            src_ref=block(send, j),
            dst_ref=block(recv, j),
            send_sem=send_sem.at[j],
            recv_sem=recv_sem.at[j],
            device_id=at(partner(j)),
            device_id_type=MESH,
        )

    def view_copy(src, dst, sem, device):
        return pltpu.make_async_remote_copy(
            src_ref=src,
            dst_ref=dst,
            send_sem=ag_send.at[sem],
            recv_sem=ag_recv.at[sem],
            device_id=device,
            device_id_type=MESH,
        )

    to_right = [
        view_copy(proj_hbm.at[c], pbuf.at[c, pl.ds(64, 64)], c, right) for c in range(2)
    ]
    to_left = [
        view_copy(proj_hbm.at[c], pbuf.at[c, pl.ds(192, 64)], 2 + c, left) for c in range(2)
    ]
    on_right = view_copy(pbuf.at[0, pl.ds(64, 64)], pbuf.at[0, pl.ds(128, 64)], 4, right)
    on_left = view_copy(pbuf.at[1, pl.ds(192, 64)], pbuf.at[1, pl.ds(128, 64)], 5, left)

    pl.semaphore_wait(barrier, PEERS - 1 + 3)
    to_right[0].start()
    to_left[1].start()
    to_left[0].start()
    to_right[1].start()

    def pack(group, carry):
        rows = pl.ds(pl.multiple_of(128 * group, 128), 128)
        for start in range(0, 2 * PIX, CHUNK):
            send[rows, start : start + CHUNK] = dot(
                s1[rows, :], x_ref[:, start : start + CHUNK]
            ).astype(jnp.bfloat16)
        for start in range(0, PIX, CHUNK):
            pair = jnp.concatenate(
                [x_ref[:, start : start + CHUNK], x_ref[:, PIX + start : PIX + start + CHUNK]], axis=0
            )
            send[rows, 2 * PIX + start : 2 * PIX + start + CHUNK] = dot(s2[rows, :], pair).astype(
                jnp.bfloat16
            )
        send[rows, 6144:6272] = dot(s1[rows, :], meta_ref[...]).astype(jnp.bfloat16)
        send[rows, 6272:6400] = dot(s2[rows, 0:128], meta_ref[...]).astype(jnp.bfloat16)

        def launch(j, inner):
            @pl.when(j > 0)
            def _():
                row_copy(j).start()

            return inner

        return lax.fori_loop(8 * group, 8 * group + 8, launch, carry)

    lax.fori_loop(0, 4, pack, 0)
    recv[0:16, :] = send[0:16, :]

    weight_rows = ctf_ref[...] / sig_ref[...]
    damping = weight_rows * ctf_ref[...]
    wtab[...] = jnp.zeros_like(wtab)
    pentab[...] = jnp.zeros_like(pentab)
    for part, piece in enumerate(split3(weight_rows)):
        wtab[16 * part : 16 * part + 16, :] = piece

    to_right[0].wait_recv()
    on_right.start()
    to_left[1].wait_recv()
    on_left.start()
    for copy in own_copies:
        copy.wait()
    to_right[1].wait_recv()
    to_left[0].wait_recv()
    on_right.wait_recv()
    on_left.wait_recv()

    for c in range(2):
        penalty = jnp.zeros((16, 256), jnp.float32)
        for start in range(0, PIX, CHUNK):
            real = pbuf[c, :, start : start + CHUNK].astype(jnp.float32)
            imag = pbuf[c, :, PIX + start : PIX + start + CHUNK].astype(jnp.float32)
            penalty = penalty + lax.dot_general(
                damping[:, start : start + CHUNK],
                real * real + imag * imag,
                (((1,), (1,)), ((), ())),
                precision=lax.Precision.HIGHEST,
                preferred_element_type=jnp.float32,
            )
        for part, piece in enumerate(split3(-0.5 * penalty)):
            pentab[c, 16 * part : 16 * part + 16, :] = piece

    lanes = lax.broadcasted_iota(jnp.int32, (48, 256), 1)
    key64 = lax.rem(lanes, 64).astype(jnp.float32)
    key16 = lax.rem(lax.broadcasted_iota(jnp.int32, (96, 128), 1), 16).astype(jnp.float32)
    stat_lane = lax.broadcasted_iota(jnp.int32, (48, 128), 1)

    def stat_rows(ref, j):
        return ref.at[pl.ds(pl.multiple_of(24 * j, 8), 24), :]

    def stat_copy(j):
        return pltpu.make_async_remote_copy(
            src_ref=stat_rows(stat_out, j),
            dst_ref=stat_rows(stat_in, j),
            send_sem=back_send.at[j],
            recv_sem=back_recv.at[j],
            device_id=at(partner(j)),
            device_id_type=MESH,
        )

    def step(g, carry):
        def arrive(j, inner):
            @pl.when(j > 0)
            def _():
                row_copy(j).wait_recv()

            return inner

        lax.fori_loop(4 * g, 4 * g + 4, arrive, 0)
        rows = pl.ds(pl.multiple_of(64 * g, 64), 64)
        notes = dot(
            perm_ref[0],
            jnp.concatenate([recv[rows, 6144:6272], recv[rows, 6272:6400]], axis=0),
        )
        group_rows = flag(notes[:, 27:28] == key16)
        for c in range(2):
            for t in range(TRANS):
                at_row = c * 432 + t * 48
                oh_s[at_row : at_row + 48, :] = flag(notes[48 * c : 48 * c + 48, t : t + 1] == key64)
        acc[...] = jnp.zeros_like(acc)

        def piece(q, inner):
            base = pl.multiple_of(q * CHUNK, CHUNK)
            here = pl.ds(base, CHUNK)
            there = pl.ds(pl.multiple_of(PIX + base, CHUNK), CHUNK)
            extra = recv[rows, pl.ds(pl.multiple_of(2 * PIX + base, CHUNK), CHUNK)]
            weights = dot(group_rows, wtab[:, here])
            real = weights * dot(perm_ref[0], jnp.concatenate([recv[rows, here], extra], axis=0))
            imag = weights * dot(perm_ref[1], jnp.concatenate([recv[rows, there], extra], axis=0))
            cos_s[...] = dot(oh_s[...], trig[:, here])
            sin_s[...] = dot(oh_s[...], trig[:, there])
            for c in range(2):
                wr = real[48 * c : 48 * c + 48]
                wi = imag[48 * c : 48 * c + 48]
                for t in range(TRANS):
                    at_row = c * 432 + t * 48
                    cosine = cos_s[at_row : at_row + 48, :]
                    sine = sin_s[at_row : at_row + 48, :]
                    a_re[at_row : at_row + 48, :] = (wr * cosine + wi * sine).astype(jnp.bfloat16)
                    a_im[at_row : at_row + 48, :] = (wi * cosine - wr * sine).astype(jnp.bfloat16)
            for c in range(2):
                mine = slice(432 * c, 432 * c + 432)
                acc[mine, :] += dot_nt(a_re[mine, :], pbuf[c, :, here]) + dot_nt(
                    a_im[mine, :], pbuf[c, :, there]
                )
            return inner

        lax.fori_loop(0, PIX // CHUNK, piece, 0)

        for c in range(2):
            penalty = dot(group_rows[48 * c : 48 * c + 48], pentab[c])
            top = acc[c * 432 : c * 432 + 48, :] + penalty
            for t in range(1, TRANS):
                at_row = c * 432 + t * 48
                top = jnp.maximum(top, acc[at_row : at_row + 48, :] + penalty)
            highest = jnp.max(top, axis=1, keepdims=True)
            offset = penalty - highest
            total = jnp.zeros((48, 256), jnp.float32)
            sum_x = jnp.zeros((48, 256), jnp.float32)
            sum_y = jnp.zeros((48, 256), jnp.float32)
            for t in range(TRANS):
                at_row = c * 432 + t * 48
                term = jnp.exp(acc[at_row : at_row + 48, :] + offset)
                total = total + term
                sum_x = sum_x + term * notes[48 * c : 48 * c + 48, 9 + t : 10 + t]
                sum_y = sum_y + term * notes[48 * c : 48 * c + 48, 18 + t : 19 + t]
            total = jnp.sum(total, axis=1, keepdims=True)
            mean_x = jnp.sum(sum_x, axis=1, keepdims=True) / total
            mean_y = jnp.sum(sum_y, axis=1, keepdims=True) / total
            log_weight = highest + jnp.log(total)
            stats = jnp.where(
                stat_lane == 0, log_weight, jnp.where(stat_lane == 1, mean_x, mean_y)
            )
            for s in range(4):
                spot = pl.ds(96 * g + 24 * s + CAP * c, CAP)
                stat_out[spot, :] = stats[CAP * s : CAP * s + CAP, :]

        def give_back(j, inner):
            @pl.when(j > 0)
            def _():
                stat_copy(j).start()

            return inner

        lax.fori_loop(4 * g, 4 * g + 4, give_back, 0)
        return carry

    lax.fori_loop(0, PEERS // 4, step, 0)
    stat_in[0:24, :] = stat_out[0:24, :]

    class_lanes = lax.broadcasted_iota(jnp.int32, (128, 64), 1)
    hot = [class_lanes == cand_ref[:, k : k + 1] for k in range(2)]
    after = flag(
        lax.broadcasted_iota(jnp.int32, (128, 128), 1)
        < lax.broadcasted_iota(jnp.int32, (128, 128), 0)
    )
    ranks = dot(after, flag(hot[0] | hot[1]))
    spots = []
    for k in range(2):
        rank = jnp.sum(jnp.where(hot[k], ranks, 0.0), axis=1, keepdims=True).astype(jnp.int32)
        owner = cand_ref[:, k : k + 1] // 2
        dc = lax.rem(lax.rem(owner, 2) + core, 2)
        oy, oz = lax.rem(owner // 2, 4), owner // 8
        dy, dz = flip(oy, my), flip(oz, mz)
        turn = lax.rem(dz - dy + 4, 4)
        j = turn * 8 + dy * 2 + dc
        spots.append(24 * j + CAP * lax.rem(cand_ref[:, k : k + 1], 2) + rank)
    stat_cols = lax.broadcasted_iota(jnp.int32, (128, 24 * PEERS), 1)
    finder = jnp.concatenate([flag(stat_cols == spot) for spot in spots], axis=0)

    def returned(j, inner):
        stat_copy(j).wait_recv()
        return inner

    lax.fori_loop(1, PEERS, returned, 0)
    parts = split3(stat_in[...])
    found = dot(finder, parts[0]) + dot(finder, parts[1]) + dot(finder, parts[2])
    logs = [found[0:128, 0:1], found[128:256, 0:1]]
    peak = jnp.maximum(logs[0], logs[1])
    raw = [jnp.exp(logs[0] - peak), jnp.exp(logs[1] - peak)]
    whole = raw[0] + raw[1]
    probs = [raw[0] / whole, raw[1] / whole]
    two = lax.broadcasted_iota(jnp.int32, (128, 2), 1)
    prob_ref[...] = jnp.where(two == 0, probs[0], probs[1])
    mean_ref[...] = jnp.where(
        two == 0,
        probs[0] * found[0:128, 1:2] + probs[1] * found[128:256, 1:2],
        probs[0] * found[0:128, 2:3] + probs[1] * found[128:256, 2:3],
    )

    def finish(j, inner):
        row_copy(j).wait_send()
        stat_copy(j).wait_send()
        return inner

    lax.fori_loop(1, PEERS, finish, 0)
    for copy in to_right + to_left + [on_right, on_left]:
        copy.wait_send()


def on_device(particles, candidates, ctf_ids, offsets, ctf_table, sigma_sq, projections):
    shift_x, shift_y = offsets[:, 0, :], offsets[:, 1, :]
    notes = jnp.concatenate(
        [(shift_x + 3) * 7 + shift_y + 3, shift_x, shift_y, ctf_ids[:, None]], axis=1
    )
    notes = jnp.pad(notes, ((0, 0), (0, 128 - notes.shape[1]))).astype(jnp.bfloat16)
    vmem = pl.BlockSpec(memory_space=pltpu.VMEM)
    hbm = pl.BlockSpec(memory_space=pl.ANY)
    out = jax.ShapeDtypeStruct((128, 2), jnp.float32)
    f32, bf16 = jnp.float32, jnp.bfloat16
    dma = pltpu.SemaphoreType.DMA
    return pl.pallas_call(
        kernel,
        out_shape=(out, out),
        in_specs=[vmem] * 7 + [hbm] * 2,
        out_specs=(vmem, vmem),
        scratch_shapes=[
            pltpu.VMEM((16 * PEERS, WIDE), bf16),
            pltpu.VMEM((16 * PEERS, WIDE), bf16),
            pltpu.VMEM((2, 256, 2 * PIX), bf16),
            pltpu.VMEM((256, 2 * PIX), bf16),
            pltpu.VMEM((64, 128), f32),
            pltpu.VMEM((16 * PEERS, 128), bf16),
            pltpu.VMEM((16 * PEERS, 256), bf16),
            pltpu.VMEM((128, PIX), bf16),
            pltpu.VMEM((2, 128, 256), bf16),
            pltpu.VMEM((ROWS, 256), bf16),
            pltpu.VMEM((ROWS, CHUNK), f32),
            pltpu.VMEM((ROWS, CHUNK), f32),
            pltpu.VMEM((ROWS, CHUNK), bf16),
            pltpu.VMEM((ROWS, CHUNK), bf16),
            pltpu.VMEM((ROWS, 256), f32),
            pltpu.VMEM((24 * PEERS, 128), f32),
            pltpu.VMEM((24 * PEERS, 128), f32),
            dma((PEERS,)),
            dma((PEERS,)),
            dma((PEERS,)),
            dma((PEERS,)),
            dma((6,)),
            dma((6,)),
            dma((3,)),
        ],
        compiler_params=pltpu.CompilerParams(
            collective_id=0, has_side_effects=True, vmem_limit_bytes=60 * 1024 * 1024
        ),
    )(
        particles,
        notes,
        candidates.T,
        candidates,
        ctf_table,
        sigma_sq[None, :],
        jnp.asarray(unpack_perm()),
        jnp.asarray(trig_table()),
        projections,
    )


def solution(mesh):
    in_specs = (
        P(("pose", "dom"), None),
        P(("pose", "dom"), None),
        P(("pose", "dom")),
        P(("pose", "dom"), None, None),
        P(),
        P(),
        P("pose", "dom", None),
    )
    out_specs = (P(("pose", "dom"), None), P(("pose", "dom"), None))
    return jax.shard_map(
        on_device, mesh=mesh, in_specs=in_specs, out_specs=out_specs, check_vma=False
    )
```

```python
import math

import jax
import jax.numpy as jnp
import numpy as np
from jax import lax
from jax.experimental import pallas as pl
from jax.experimental.pallas import tpu as pltpu
from jax.sharding import PartitionSpec as P

MESH = pl.DeviceIdType.MESH
BOX = 128
PIX = 2048
TRANS = 9
CAP = 12
PEERS = 32
CHUNK = 512
WIDE = 6400
ROWS = 864
AHEAD = 3
ORDER = "P0 W F G0 P1 P2 G1 P3 G2 V S0 G3 S1 G4 S2 G5 S3 S4 S5 G6 S6 G7 S7".split()


def trig_table():
    pixel = np.arange(PIX)
    kx, ky = pixel % 64 - 32, pixel // 64
    both = np.zeros((49, 2 * PIX), np.float64)
    for ox in range(-3, 4):
        for oy in range(-3, 4):
            angle = 2.0 * math.pi * ((kx * ox + ky * oy) % BOX) / BOX
            both[(ox + 3) * 7 + oy + 3] = np.concatenate([np.cos(angle), np.sin(angle)])
    table = np.zeros((256, 2 * PIX), jnp.bfloat16)
    left = both
    for part in range(3):
        piece = left.astype(jnp.bfloat16)
        table[64 * part : 64 * part + 49] = piece
        left = left - piece.astype(np.float64)
    return table


def unpack_perm():
    perm = np.zeros((2, 96, 128), np.float32)
    for m in range(48):
        src, k = divmod(m, CAP)
        perm[:, m, src * 16 + k] = 1.0
        for part in range(2):
            col = src * 16 + 12 + k if k < 4 else 64 + src * 16 + 8 * part + k - 4
            perm[part, 48 + m, col] = 1.0
    return perm.astype(jnp.bfloat16)


def dot(a, b):
    return jnp.dot(a, b, preferred_element_type=jnp.float32)


def dot_nt(a, b):
    return lax.dot_general(a, b, (((1,), (1,)), ((), ())), preferred_element_type=jnp.float32)


def split3(value):
    first = value.astype(jnp.bfloat16)
    rest = value - first.astype(jnp.float32)
    second = rest.astype(jnp.bfloat16)
    third = (rest - second.astype(jnp.float32)).astype(jnp.bfloat16)
    return first, second, third


def flag(cond):
    return jnp.where(cond, 1.0, 0.0).astype(jnp.bfloat16)


def fiota(shape, dim):
    return lax.broadcasted_iota(jnp.int32, shape, dim).astype(jnp.float32)


def kernel(
    x_hbm,
    meta_ref,
    cand_ref,
    ctf_ref,
    sig_ref,
    perm_ref,
    trig_hbm,
    proj_hbm,
    prob_ref,
    mean_ref,
    x_all,
    meta_all,
    send,
    recv,
    pbuf,
    trig,
    q_s,
    s1,
    s2,
    wtab,
    pentab,
    oh_s,
    wr_s,
    wi_s,
    a_s,
    notes_s,
    acc,
    stat_out,
    stat_in,
    send_sem,
    recv_sem,
    back_send,
    back_recv,
    ag_send,
    ag_recv,
    lap_send,
    lap_recv,
    local_sem,
):
    me = lax.axis_index("pose")
    dom = lax.axis_index("dom")
    core, my, mz = lax.rem(me, 2), lax.rem(me // 2, 4), me // 8
    along, other = mz * (1 - core) + my * core, my * (1 - core) + mz * core
    along_step, other_step = 8 - 6 * core, 2 + 6 * core

    def flip(a, b):
        hi = lax.rem(a // 2 + b // 2, 2)
        lo = lax.rem(lax.rem(a, 2) + lax.rem(b, 2), 2)
        return 2 * hi + lo

    def pose_of(place, cross, which):
        return place * along_step + cross * other_step + which

    def taker(i):
        return pose_of(along, flip(other, i // 2), lax.rem(core + lax.rem(i, 2), 2))

    def source(j):
        turn, a, c = j // 8, lax.rem(j // 2, 4), lax.rem(j, 2)
        reach = turn + (turn // 2) * (1 - 2 * lax.rem(turn, 2))
        place = (1 - c) * lax.rem(along - reach + 4, 4) + c * flip(along, a)
        cross = (1 - c) * flip(other, a) + c * lax.rem(other - reach + 4, 4)
        return pose_of(place, cross, lax.rem(core + c, 2))

    def at(p):
        return {"pose": p, "dom": dom}

    right = {"pose": me, "dom": lax.rem(dom + 1, 4)}
    left = {"pose": me, "dom": lax.rem(dom + 3, 4)}
    across = {"pose": me, "dom": lax.rem(dom + 2, 4)}

    barrier = pltpu.get_barrier_semaphore()

    def greet(j, carry):
        pl.semaphore_signal(
            barrier, inc=1, device_id=at(lax.rem(me + j, PEERS)), device_id_type=MESH
        )
        return carry

    lax.fori_loop(1, PEERS, greet, 0)
    for peer in (right, left, across):
        pl.semaphore_signal(barrier, inc=1, device_id=peer, device_id_type=MESH)

    own_copies = [
        pltpu.make_async_copy(proj_hbm.at[c], pbuf.at[c, pl.ds(0, 64)], local_sem.at[c])
        for c in range(2)
    ]
    own_copies.append(pltpu.make_async_copy(trig_hbm, trig, local_sem.at[2]))
    own_copies.append(pltpu.make_async_copy(x_hbm, x_all.at[0], local_sem.at[3]))
    for copy in own_copies[::-1]:
        copy.start()

    class_rows = fiota((64, 128), 0)
    before = flag(
        lax.broadcasted_iota(jnp.int32, (128, 128), 0)
        < lax.broadcasted_iota(jnp.int32, (128, 128), 1)
    )
    name_lanes = flag(
        lax.broadcasted_iota(jnp.int32, (16, 128), 1)
        == lax.broadcasted_iota(jnp.int32, (16, 128), 0) + 28
    )
    slot_rows = fiota((16, 128), 0)
    meta_all[0] = meta_ref[...]

    def block(ref, j):
        return ref.at[pl.ds(pl.multiple_of(16 * j, 16), 16), :]

    def row_copy(j):
        return pltpu.make_async_remote_copy(
            src_ref=block(send, j),
            dst_ref=block(recv, j),
            send_sem=send_sem.at[j],
            recv_sem=recv_sem.at[j],
            device_id=at(taker(lax.rem(j, 8))),
            device_id_type=MESH,
        )

    up = at(pose_of(lax.rem(along + 1, 4), other, core))
    down = at(pose_of(lax.rem(along + 3, 4), other, core))

    def lap_copy(src, dst, sem, device):
        return pltpu.make_async_remote_copy(
            src_ref=src,
            dst_ref=dst,
            send_sem=lap_send.at[sem],
            recv_sem=lap_recv.at[sem],
            device_id=device,
            device_id_type=MESH,
        )

    first, second = pl.ds(0, 64), pl.ds(64, 64)
    laps = [
        lap_copy(meta_all.at[0], meta_all.at[1], 0, up),
        lap_copy(x_all.at[0, first], x_all.at[1, first], 1, up),
        lap_copy(x_all.at[0, second], x_all.at[1, second], 2, up),
        lap_copy(meta_all.at[0], meta_all.at[2], 3, down),
        lap_copy(x_all.at[0, second], x_all.at[2, second], 4, down),
        lap_copy(x_all.at[0, first], x_all.at[2, first], 5, down),
        lap_copy(meta_all.at[1], meta_all.at[3], 6, up),
        lap_copy(x_all.at[1, first], x_all.at[3, first], 7, up),
        lap_copy(x_all.at[2, second], x_all.at[3, second], 8, down),
    ]

    def view_copy(src, dst, sem, device):
        return pltpu.make_async_remote_copy(
            src_ref=src,
            dst_ref=dst,
            send_sem=ag_send.at[sem],
            recv_sem=ag_recv.at[sem],
            device_id=device,
            device_id_type=MESH,
        )

    to_right = [
        view_copy(pbuf.at[c, pl.ds(0, 64)], pbuf.at[c, pl.ds(64, 64)], c, right) for c in range(2)
    ]
    to_left = [
        view_copy(pbuf.at[c, pl.ds(0, 64)], pbuf.at[c, pl.ds(192, 64)], 2 + c, left) for c in range(2)
    ]
    on_right = view_copy(pbuf.at[0, pl.ds(64, 64)], pbuf.at[0, pl.ds(128, 64)], 4, right)
    on_left = view_copy(pbuf.at[1, pl.ds(192, 64)], pbuf.at[1, pl.ds(128, 64)], 5, left)

    pl.semaphore_wait(barrier, PEERS - 1 + 3)
    own_copies[3].wait()
    for k in (0, 1, 3, 4):
        laps[k].start()
    own_copies[0].wait()
    own_copies[1].wait()
    to_right[0].start()
    to_left[1].start()
    laps[2].start()
    laps[5].start()
    to_left[0].start()
    to_right[1].start()

    def pass_on(_):
        laps[0].wait_recv()
        laps[1].wait_recv()
        laps[6].start()
        laps[7].start()
        laps[4].wait_recv()
        laps[8].start()

    def pack(b):
        @pl.when(b == 1)
        def _():
            laps[2].wait_recv()

        @pl.when(b == 2)
        def _():
            laps[3].wait_recv()
            laps[5].wait_recv()

        @pl.when(b == 3)
        def _():
            for lap in laps[6:]:
                lap.wait_recv()

        notes = meta_all[b]
        names = dot_nt(name_lanes, notes)
        named = (class_rows == names[0:1, :]) | (class_rows == names[1:2, :])
        q_s[...] = jnp.where(named, dot(flag(named), before), -1.0)
        for i in range(8):
            p = taker(i)
            qa = q_s[pl.ds(2 * p, 1), :]
            qb = q_s[pl.ds(2 * p + 1, 1), :]
            rows = slice(16 * i, 16 * i + 16)
            s1[rows, :] = flag(
                jnp.where(slot_rows < 12.0, qa, qb)
                == jnp.where(slot_rows < 12.0, slot_rows, slot_rows - 12.0)
            )
            s2[rows, 0:128] = flag((qb == slot_rows + 4.0) & (slot_rows < 8.0))
            s2[rows, 128:256] = flag((qb == slot_rows - 4.0) & (slot_rows >= 8.0))
        rows = pl.ds(pl.multiple_of(128 * b, 128), 128)
        for start in range(0, 2 * PIX, CHUNK):
            send[rows, start : start + CHUNK] = dot(
                s1[...], x_all[b, :, start : start + CHUNK]
            ).astype(jnp.bfloat16)
        for start in range(0, PIX, CHUNK):
            pair = jnp.concatenate(
                [
                    x_all[b, :, start : start + CHUNK],
                    x_all[b, :, PIX + start : PIX + start + CHUNK],
                ],
                axis=0,
            )
            send[rows, 2 * PIX + start : 2 * PIX + start + CHUNK] = dot(s2[...], pair).astype(
                jnp.bfloat16
            )
        send[rows, 6144:6272] = dot(s1[...], notes).astype(jnp.bfloat16)
        send[rows, 6272:6400] = dot(s2[:, 0:128], notes).astype(jnp.bfloat16)

        def launch(i, inner):
            row_copy(8 * b + i).start()
            return inner

        lax.fori_loop(1, 8, launch, 0)
        mine = pl.ds(pl.multiple_of(128 * b, 128), 16)
        recv[mine, :] = send[mine, :]

    weight_rows = ctf_ref[...] / sig_ref[...]
    damping = weight_rows * ctf_ref[...]
    wtab[...] = jnp.zeros_like(wtab)
    pentab[...] = jnp.zeros_like(pentab)
    for part, piece in enumerate(split3(weight_rows)):
        wtab[16 * part : 16 * part + 16, :] = piece

    own_copies[2].wait()

    def forward(_):
        to_right[0].wait_recv()
        on_right.start()
        to_left[1].wait_recv()
        on_left.start()

    def whole_views(_):
        to_right[1].wait_recv()
        to_left[0].wait_recv()
        on_right.wait_recv()
        on_left.wait_recv()

        for c in range(2):
            penalty = jnp.zeros((16, 256), jnp.float32)
            for start in range(0, PIX, CHUNK):
                real = pbuf[c, :, start : start + CHUNK].astype(jnp.float32)
                imag = pbuf[c, :, PIX + start : PIX + start + CHUNK].astype(jnp.float32)
                penalty = penalty + lax.dot_general(
                    damping[:, start : start + CHUNK],
                    real * real + imag * imag,
                    (((1,), (1,)), ((), ())),
                    precision=lax.Precision.HIGHEST,
                    preferred_element_type=jnp.float32,
                )
            for part, piece in enumerate(split3(-0.5 * penalty)):
                pentab[c, 16 * part : 16 * part + 16, :] = piece

    lanes = lax.broadcasted_iota(jnp.int32, (48, 256), 1)
    key64 = lax.rem(lanes, 64).astype(jnp.float32)
    key16 = lax.rem(lax.broadcasted_iota(jnp.int32, (96, 128), 1), 16).astype(jnp.float32)
    stat_lane = lax.broadcasted_iota(jnp.int32, (48, 128), 1)

    def stat_rows(ref, j):
        return ref.at[pl.ds(pl.multiple_of(24 * j, 8), 24), :]

    def stat_copy(j):
        return pltpu.make_async_remote_copy(
            src_ref=stat_rows(stat_out, j),
            dst_ref=stat_rows(stat_in, j),
            send_sem=back_send.at[j],
            recv_sem=back_recv.at[j],
            device_id=at(source(j)),
            device_id_type=MESH,
        )

    def shift_rows(g):
        def arrive(j, inner):
            @pl.when(lax.rem(j, 8) > 0)
            def _():
                row_copy(j).wait_recv()

            return inner

        lax.fori_loop(4 * g, 4 * g + 4, arrive, 0)
        slot = lax.rem(g, AHEAD)
        rows = pl.ds(pl.multiple_of(64 * g, 64), 64)
        notes = dot(
            perm_ref[0],
            jnp.concatenate([recv[rows, 6144:6272], recv[rows, 6272:6400]], axis=0),
        )
        notes_s[slot] = notes
        group_rows = flag(notes[:, 27:28] == key16)
        for c in range(2):
            for t in range(TRANS):
                at_row = c * 432 + t * 48
                oh_s[at_row : at_row + 48, :] = flag(notes[48 * c : 48 * c + 48, t : t + 1] == key64)
        for base in range(0, PIX, CHUNK):
            here = slice(base, base + CHUNK)
            extra = recv[rows, 2 * PIX + base : 2 * PIX + base + CHUNK]
            weights = dot(group_rows, wtab[:, here])
            real = jnp.concatenate([recv[rows, here], extra], axis=0)
            imag = jnp.concatenate([recv[rows, PIX + base : PIX + base + CHUNK], extra], axis=0)
            wr_s[:, here] = weights * dot(perm_ref[0], real)
            wi_s[:, here] = weights * dot(perm_ref[1], imag)
        for base in range(0, PIX, CHUNK):
            here = slice(base, base + CHUNK)
            there = slice(PIX + base, PIX + base + CHUNK)
            cosines = dot(oh_s[...], trig[:, here])
            sines = dot(oh_s[...], trig[:, there])
            for c in range(2):
                wr = wr_s[48 * c : 48 * c + 48, here]
                wi = wi_s[48 * c : 48 * c + 48, here]
                for t in range(TRANS):
                    at_row = c * 432 + t * 48
                    span = slice(at_row, at_row + 48)
                    cosine, sine = cosines[span], sines[span]
                    a_s[slot, span, here] = (wr * cosine + wi * sine).astype(jnp.bfloat16)
                    a_s[slot, span, there] = (wi * cosine - wr * sine).astype(jnp.bfloat16)

    def score(g):
        slot = lax.rem(g, AHEAD)
        notes = notes_s[slot]
        group_rows = flag(notes[:, 27:28] == key16)
        for c in range(2):
            acc[432 * c : 432 * c + 432, :] = dot_nt(a_s[slot, 432 * c : 432 * c + 432, :], pbuf[c])
        for c in range(2):
            penalty = dot(group_rows[48 * c : 48 * c + 48], pentab[c])
            top = acc[c * 432 : c * 432 + 48, :] + penalty
            for t in range(1, TRANS):
                at_row = c * 432 + t * 48
                top = jnp.maximum(top, acc[at_row : at_row + 48, :] + penalty)
            highest = jnp.max(top, axis=1, keepdims=True)
            offset = penalty - highest
            total = jnp.zeros((48, 256), jnp.float32)
            sum_x = jnp.zeros((48, 256), jnp.float32)
            sum_y = jnp.zeros((48, 256), jnp.float32)
            for t in range(TRANS):
                at_row = c * 432 + t * 48
                term = jnp.exp(acc[at_row : at_row + 48, :] + offset)
                total = total + term
                sum_x = sum_x + term * notes[48 * c : 48 * c + 48, 9 + t : 10 + t]
                sum_y = sum_y + term * notes[48 * c : 48 * c + 48, 18 + t : 19 + t]
            total = jnp.sum(total, axis=1, keepdims=True)
            mean_x = jnp.sum(sum_x, axis=1, keepdims=True) / total
            mean_y = jnp.sum(sum_y, axis=1, keepdims=True) / total
            log_weight = highest + jnp.log(total)
            stats = jnp.where(
                stat_lane == 0, log_weight, jnp.where(stat_lane == 1, mean_x, mean_y)
            )
            for s in range(4):
                spot = pl.ds(96 * g + 24 * s + CAP * c, CAP)
                stat_out[spot, :] = stats[CAP * s : CAP * s + CAP, :]

        def give_back(j, inner):
            @pl.when(j > 0)
            def _():
                stat_copy(j).start()

            return inner

        lax.fori_loop(4 * g, 4 * g + 4, give_back, 0)

    def turn(v, carry):
        def chosen(kind):
            spots = [at_v for at_v, op in enumerate(ORDER) if op[0] == kind]
            here, arg = v == spots[0], int(ORDER[spots[0]][1:] or 0)
            for at_v in spots[1:]:
                arg = jnp.where(v == at_v, int(ORDER[at_v][1:] or 0), arg)
                here = here | (v == at_v)
            return here, arg

        for kind, work in (
            ("P", pack),
            ("W", pass_on),
            ("F", forward),
            ("G", shift_rows),
            ("V", whole_views),
            ("S", score),
        ):
            here, arg = chosen(kind)

            @pl.when(here)
            def _(work=work, arg=arg):
                work(arg)

        return carry

    lax.fori_loop(0, len(ORDER), turn, 0)
    stat_in[0:24, :] = stat_out[0:24, :]

    class_lanes = lax.broadcasted_iota(jnp.int32, (128, 64), 1)
    hot = [class_lanes == cand_ref[:, k : k + 1] for k in range(2)]
    after = flag(
        lax.broadcasted_iota(jnp.int32, (128, 128), 1)
        < lax.broadcasted_iota(jnp.int32, (128, 128), 0)
    )
    ranks = dot(after, flag(hot[0] | hot[1]))
    spots = []
    for k in range(2):
        rank = jnp.sum(jnp.where(hot[k], ranks, 0.0), axis=1, keepdims=True).astype(jnp.int32)
        owner = cand_ref[:, k : k + 1] // 2
        dc = lax.rem(lax.rem(owner, 2) + core, 2)
        oy, oz = lax.rem(owner // 2, 4), owner // 8
        place = oz * (1 - core) + oy * core
        cross = oy * (1 - core) + oz * core
        ahead = lax.rem(place - along + 4, 4)
        b = jnp.where(ahead == 3, 2, jnp.where(ahead == 2, 3, ahead))
        j = b * 8 + flip(cross, other) * 2 + dc
        spots.append(24 * j + CAP * lax.rem(cand_ref[:, k : k + 1], 2) + rank)
    stat_cols = lax.broadcasted_iota(jnp.int32, (128, 24 * PEERS), 1)
    finder = jnp.concatenate([flag(stat_cols == spot) for spot in spots], axis=0)

    def returned(j, inner):
        stat_copy(j).wait_recv()
        return inner

    lax.fori_loop(1, PEERS, returned, 0)
    parts = split3(stat_in[...])
    found = dot(finder, parts[0]) + dot(finder, parts[1]) + dot(finder, parts[2])
    logs = [found[0:128, 0:1], found[128:256, 0:1]]
    peak = jnp.maximum(logs[0], logs[1])
    raw = [jnp.exp(logs[0] - peak), jnp.exp(logs[1] - peak)]
    whole = raw[0] + raw[1]
    probs = [raw[0] / whole, raw[1] / whole]
    two = lax.broadcasted_iota(jnp.int32, (128, 2), 1)
    prob_ref[...] = jnp.where(two == 0, probs[0], probs[1])
    mean_ref[...] = jnp.where(
        two == 0,
        probs[0] * found[0:128, 1:2] + probs[1] * found[128:256, 1:2],
        probs[0] * found[0:128, 2:3] + probs[1] * found[128:256, 2:3],
    )

    def finish(j, inner):
        @pl.when(lax.rem(j, 8) > 0)
        def _():
            row_copy(j).wait_send()

        stat_copy(j).wait_send()
        return inner

    lax.fori_loop(1, PEERS, finish, 0)
    for copy in to_right + to_left + [on_right, on_left] + laps:
        copy.wait_send()


def on_device(particles, candidates, ctf_ids, offsets, ctf_table, sigma_sq, projections):
    shift_x, shift_y = offsets[:, 0, :], offsets[:, 1, :]
    notes = jnp.concatenate(
        [(shift_x + 3) * 7 + shift_y + 3, shift_x, shift_y, ctf_ids[:, None], candidates], axis=1
    )
    notes = jnp.pad(notes, ((0, 0), (0, 128 - notes.shape[1]))).astype(jnp.bfloat16)
    vmem = pl.BlockSpec(memory_space=pltpu.VMEM)
    hbm = pl.BlockSpec(memory_space=pl.ANY)
    out = jax.ShapeDtypeStruct((128, 2), jnp.float32)
    f32, bf16 = jnp.float32, jnp.bfloat16
    dma = pltpu.SemaphoreType.DMA
    return pl.pallas_call(
        kernel,
        out_shape=(out, out),
        in_specs=[hbm] + [vmem] * 5 + [hbm] * 2,
        out_specs=(vmem, vmem),
        scratch_shapes=[
            pltpu.VMEM((4, 128, 2 * PIX), bf16),
            pltpu.VMEM((4, 128, 128), bf16),
            pltpu.VMEM((16 * PEERS, WIDE), bf16),
            pltpu.VMEM((16 * PEERS, WIDE), bf16),
            pltpu.VMEM((2, 256, 2 * PIX), bf16),
            pltpu.VMEM((256, 2 * PIX), bf16),
            pltpu.VMEM((64, 128), f32),
            pltpu.VMEM((128, 128), bf16),
            pltpu.VMEM((128, 256), bf16),
            pltpu.VMEM((128, PIX), bf16),
            pltpu.VMEM((2, 128, 256), bf16),
            pltpu.VMEM((ROWS, 256), bf16),
            pltpu.VMEM((96, PIX), f32),
            pltpu.VMEM((96, PIX), f32),
            pltpu.VMEM((AHEAD, ROWS, 2 * PIX), bf16),
            pltpu.VMEM((AHEAD, 96, 128), f32),
            pltpu.VMEM((ROWS, 256), f32),
            pltpu.VMEM((24 * PEERS, 128), f32),
            pltpu.VMEM((24 * PEERS, 128), f32),
            dma((PEERS,)),
            dma((PEERS,)),
            dma((PEERS,)),
            dma((PEERS,)),
            dma((6,)),
            dma((6,)),
            dma((9,)),
            dma((9,)),
            dma((4,)),
        ],
        compiler_params=pltpu.CompilerParams(
            collective_id=0, has_side_effects=True, vmem_limit_bytes=60 * 1024 * 1024
        ),
    )(
        particles,
        notes,
        candidates,
        ctf_table,
        sigma_sq[None, :],
        jnp.asarray(unpack_perm()),
        jnp.asarray(trig_table()),
        projections,
    )


def solution(mesh):
    in_specs = (
        P(("pose", "dom"), None),
        P(("pose", "dom"), None),
        P(("pose", "dom")),
        P(("pose", "dom"), None, None),
        P(),
        P(),
        P("pose", "dom", None),
    )
    out_specs = (P(("pose", "dom"), None), P(("pose", "dom"), None))
    return jax.shard_map(
        on_device, mesh=mesh, in_specs=in_specs, out_specs=out_specs, check_vma=False
    )
```

```python
import math

import jax
import jax.numpy as jnp
import numpy as np
from jax import lax
from jax.experimental import pallas as pl
from jax.experimental.pallas import tpu as pltpu
from jax.sharding import PartitionSpec as P

MESH = pl.DeviceIdType.MESH
BOX = 128
PIX = 2048
TRANS = 9
CAP = 12
PEERS = 32
CHUNK = 512
WIDE = 6400
ROWS = 864
AHEAD = 4
ORDER = "P0 K G0 W F0 V0 S0 P1 P2 G1 F1 S2 P3 G2 S4 G3 S6 V1 S1 S3 S5 S7 G4 S8 S9 G5 S10 S11 G6 S12 S13 G7 S14 S15".split()


def trig_table():
    pixel = np.arange(PIX)
    kx, ky = pixel % 64 - 32, pixel // 64
    both = np.zeros((49, 2 * PIX), np.float64)
    for ox in range(-3, 4):
        for oy in range(-3, 4):
            angle = 2.0 * math.pi * ((kx * ox + ky * oy) % BOX) / BOX
            both[(ox + 3) * 7 + oy + 3] = np.concatenate([np.cos(angle), np.sin(angle)])
    table = np.zeros((256, 2 * PIX), jnp.bfloat16)
    left = both
    for part in range(3):
        piece = left.astype(jnp.bfloat16)
        table[64 * part : 64 * part + 49] = piece
        left = left - piece.astype(np.float64)
    return table


def unpack_perm():
    perm = np.zeros((2, 96, 128), np.float32)
    for m in range(48):
        src, k = divmod(m, CAP)
        perm[:, m, src * 16 + k] = 1.0
        for part in range(2):
            col = src * 16 + 12 + k if k < 4 else 64 + src * 16 + 8 * part + k - 4
            perm[part, 48 + m, col] = 1.0
    return perm.astype(jnp.bfloat16)


def dot(a, b):
    return jnp.dot(a, b, preferred_element_type=jnp.float32)


def dot_nt(a, b):
    return lax.dot_general(a, b, (((1,), (1,)), ((), ())), preferred_element_type=jnp.float32)


def split3(value):
    first = value.astype(jnp.bfloat16)
    rest = value - first.astype(jnp.float32)
    second = rest.astype(jnp.bfloat16)
    third = (rest - second.astype(jnp.float32)).astype(jnp.bfloat16)
    return first, second, third


def flag(cond):
    return jnp.where(cond, 1.0, 0.0).astype(jnp.bfloat16)


def fiota(shape, dim):
    return lax.broadcasted_iota(jnp.int32, shape, dim).astype(jnp.float32)


def kernel(
    x_hbm,
    cand_ref,
    ids_ref,
    off_ref,
    ctf_ref,
    sig_ref,
    perm_ref,
    trig_hbm,
    proj_hbm,
    out_ref,
    x_all,
    note_s,
    finder,
    meta_all,
    send,
    recv,
    pbuf,
    trig,
    q_s,
    s1,
    s2,
    wtab,
    pentab,
    oh_s,
    wr_s,
    wi_s,
    a_s,
    notes_s,
    acc,
    stat_out,
    stat_in,
    send_sem,
    recv_sem,
    back_send,
    back_recv,
    ag_send,
    ag_recv,
    lap_send,
    lap_recv,
    local_sem,
):
    me = lax.axis_index("pose")
    dom = lax.axis_index("dom")
    core, my, mz = lax.rem(me, 2), lax.rem(me // 2, 4), me // 8
    along, other = mz * (1 - core) + my * core, my * (1 - core) + mz * core
    along_step, other_step = 8 - 6 * core, 2 + 6 * core

    def flip(a, b):
        hi = lax.rem(a // 2 + b // 2, 2)
        lo = lax.rem(lax.rem(a, 2) + lax.rem(b, 2), 2)
        return 2 * hi + lo

    def pose_of(place, cross, which):
        return place * along_step + cross * other_step + which

    def taker(i):
        return pose_of(along, flip(other, i // 2), lax.rem(core + lax.rem(i, 2), 2))

    def source(j):
        turn, a, c = j // 8, lax.rem(j // 2, 4), lax.rem(j, 2)
        reach = turn + (turn // 2) * (1 - 2 * lax.rem(turn, 2))
        place = (1 - c) * lax.rem(along - reach + 4, 4) + c * flip(along, a)
        cross = (1 - c) * flip(other, a) + c * lax.rem(other - reach + 4, 4)
        return pose_of(place, cross, lax.rem(core + c, 2))

    def at(p):
        return {"pose": p, "dom": dom}

    right = {"pose": me, "dom": lax.rem(dom + 1, 4)}
    left = {"pose": me, "dom": lax.rem(dom + 3, 4)}
    across = {"pose": me, "dom": lax.rem(dom + 2, 4)}

    barrier = pltpu.get_barrier_semaphore()

    def greet(j, carry):
        pl.semaphore_signal(
            barrier, inc=1, device_id=at(lax.rem(me + j, PEERS)), device_id_type=MESH
        )
        return carry

    lax.fori_loop(1, PEERS, greet, 0)
    for peer in (right, left, across):
        pl.semaphore_signal(barrier, inc=1, device_id=peer, device_id_type=MESH)

    own_copies = [
        pltpu.make_async_copy(proj_hbm.at[c], pbuf.at[c, pl.ds(0, 64)], local_sem.at[c])
        for c in range(2)
    ]
    own_copies.append(pltpu.make_async_copy(trig_hbm, trig, local_sem.at[2]))
    own_copies.append(pltpu.make_async_copy(x_hbm, x_all.at[0], local_sem.at[3]))
    for copy in own_copies[::-1]:
        copy.start()

    class_rows = fiota((64, 128), 0)
    before = flag(
        lax.broadcasted_iota(jnp.int32, (128, 128), 0)
        < lax.broadcasted_iota(jnp.int32, (128, 128), 1)
    )
    name_lanes = flag(
        lax.broadcasted_iota(jnp.int32, (16, 128), 1)
        == lax.broadcasted_iota(jnp.int32, (16, 128), 0) + 28
    )
    slot_rows = fiota((16, 128), 0)
    note_s[...] = jnp.zeros_like(note_s)
    for t in range(TRANS):
        shift_x = off_ref[t, 0:1, :].astype(jnp.float32)
        shift_y = off_ref[t, 1:2, :].astype(jnp.float32)
        note_s[t : t + 1, :] = (shift_x + 3.0) * 7.0 + shift_y + 3.0
        note_s[9 + t : 10 + t, :] = shift_x
        note_s[18 + t : 19 + t, :] = shift_y
    note_s[27:28, :] = ids_ref[...].astype(jnp.float32)
    note_s[28:30, :] = cand_ref[...].astype(jnp.float32)
    meta_all[0] = note_s[...].T.astype(jnp.bfloat16)

    def block(ref, j):
        return ref.at[pl.ds(pl.multiple_of(16 * j, 16), 16), :]

    def row_copy(j):
        return pltpu.make_async_remote_copy(
            src_ref=block(send, j),
            dst_ref=block(recv, j),
            send_sem=send_sem.at[j],
            recv_sem=recv_sem.at[j],
            device_id=at(taker(lax.rem(j, 8))),
            device_id_type=MESH,
        )

    up = at(pose_of(lax.rem(along + 1, 4), other, core))
    down = at(pose_of(lax.rem(along + 3, 4), other, core))

    def lap_copy(src, dst, sem, device):
        return pltpu.make_async_remote_copy(
            src_ref=src,
            dst_ref=dst,
            send_sem=lap_send.at[sem],
            recv_sem=lap_recv.at[sem],
            device_id=device,
            device_id_type=MESH,
        )

    first, second = pl.ds(0, 64), pl.ds(64, 64)
    laps = [
        lap_copy(meta_all.at[0], meta_all.at[1], 0, up),
        lap_copy(x_all.at[0, first], x_all.at[1, first], 1, up),
        lap_copy(x_all.at[0, second], x_all.at[1, second], 2, up),
        lap_copy(meta_all.at[0], meta_all.at[2], 3, down),
        lap_copy(x_all.at[0, second], x_all.at[2, second], 4, down),
        lap_copy(x_all.at[0, first], x_all.at[2, first], 5, down),
        lap_copy(meta_all.at[1], meta_all.at[3], 6, up),
        lap_copy(x_all.at[1, first], x_all.at[3, first], 7, up),
        lap_copy(x_all.at[2, second], x_all.at[3, second], 8, down),
    ]

    def view_copy(src, dst, sem, device):
        return pltpu.make_async_remote_copy(
            src_ref=src,
            dst_ref=dst,
            send_sem=ag_send.at[sem],
            recv_sem=ag_recv.at[sem],
            device_id=device,
            device_id_type=MESH,
        )

    def own_right(c):
        return view_copy(pbuf.at[c, pl.ds(0, 64)], pbuf.at[c, pl.ds(64, 64)], c, right)

    def own_left(c):
        return view_copy(pbuf.at[c, pl.ds(0, 64)], pbuf.at[c, pl.ds(192, 64)], 2 + c, left)

    def on_right(c):
        return view_copy(pbuf.at[c, pl.ds(64, 32)], pbuf.at[c, pl.ds(128, 32)], 4 + c, right)

    def on_left(c):
        return view_copy(pbuf.at[c, pl.ds(224, 32)], pbuf.at[c, pl.ds(160, 32)], 6 + c, left)

    pl.semaphore_wait(barrier, PEERS - 1 + 3)
    own_copies[3].wait()
    for k in (0, 1, 3, 4):
        laps[k].start()
    own_copies[0].wait()
    own_copies[1].wait()
    own_right(0).start()
    own_left(0).start()
    laps[2].start()
    laps[5].start()

    def pass_on(_):
        laps[0].wait_recv()
        laps[1].wait_recv()
        laps[6].start()
        laps[7].start()
        laps[4].wait_recv()
        laps[8].start()

    def pack(b):
        @pl.when(b == 1)
        def _():
            laps[2].wait_recv()

        @pl.when(b == 2)
        def _():
            laps[3].wait_recv()
            laps[5].wait_recv()

        @pl.when(b == 3)
        def _():
            for lap in laps[6:]:
                lap.wait_recv()

        notes = meta_all[b]
        names = dot_nt(name_lanes, notes)
        named = (class_rows == names[0:1, :]) | (class_rows == names[1:2, :])
        q_s[...] = jnp.where(named, dot(flag(named), before), -1.0)
        for i in range(8):
            p = taker(i)
            qa = q_s[pl.ds(2 * p, 1), :]
            qb = q_s[pl.ds(2 * p + 1, 1), :]
            rows = slice(16 * i, 16 * i + 16)
            s1[rows, :] = flag(
                jnp.where(slot_rows < 12.0, qa, qb)
                == jnp.where(slot_rows < 12.0, slot_rows, slot_rows - 12.0)
            )
            s2[rows, 0:128] = flag((qb == slot_rows + 4.0) & (slot_rows < 8.0))
            s2[rows, 128:256] = flag((qb == slot_rows - 4.0) & (slot_rows >= 8.0))
        rows = pl.ds(pl.multiple_of(128 * b, 128), 128)
        for start in range(0, 2 * PIX, CHUNK):
            send[rows, start : start + CHUNK] = dot(
                s1[...], x_all[b, :, start : start + CHUNK]
            ).astype(jnp.bfloat16)
        for start in range(0, PIX, CHUNK):
            pair = jnp.concatenate(
                [
                    x_all[b, :, start : start + CHUNK],
                    x_all[b, :, PIX + start : PIX + start + CHUNK],
                ],
                axis=0,
            )
            send[rows, 2 * PIX + start : 2 * PIX + start + CHUNK] = dot(s2[...], pair).astype(
                jnp.bfloat16
            )
        send[rows, 6144:6272] = dot(s1[...], notes).astype(jnp.bfloat16)
        send[rows, 6272:6400] = dot(s2[:, 0:128], notes).astype(jnp.bfloat16)

        def launch(i, inner):
            row_copy(8 * b + i).start()
            return inner

        lax.fori_loop(1, 8, launch, 0)
        mine = pl.ds(pl.multiple_of(128 * b, 128), 16)
        recv[mine, :] = send[mine, :]

    own_copies[2].wait()

    def forward(c):
        own_right(c).wait_recv()
        on_right(c).start()
        own_left(c).wait_recv()
        on_left(c).start()

        @pl.when(c == 0)
        def _():
            own_right(1).start()
            own_left(1).start()

    def whole_views(c):
        on_right(c).wait_recv()
        on_left(c).wait_recv()
        damping = ctf_ref[...] / sig_ref[...] * ctf_ref[...]
        penalty = jnp.zeros((16, 256), jnp.float32)
        for start in range(0, PIX, CHUNK):
            real = pbuf[c, :, start : start + CHUNK].astype(jnp.float32)
            imag = pbuf[c, :, PIX + start : PIX + start + CHUNK].astype(jnp.float32)
            penalty = penalty + lax.dot_general(
                damping[:, start : start + CHUNK],
                real * real + imag * imag,
                (((1,), (1,)), ((), ())),
                precision=lax.Precision.HIGHEST,
                preferred_element_type=jnp.float32,
            )
        for part, piece in enumerate(split3(-0.5 * penalty)):
            pentab[c, 16 * part : 16 * part + 16, :] = piece

    lanes = lax.broadcasted_iota(jnp.int32, (48, 256), 1)
    key64 = lax.rem(lanes, 64).astype(jnp.float32)
    key16 = lax.rem(lax.broadcasted_iota(jnp.int32, (96, 128), 1), 16).astype(jnp.float32)
    stat_lane = lax.broadcasted_iota(jnp.int32, (48, 128), 1)

    def stat_rows(ref, j):
        return ref.at[pl.ds(pl.multiple_of(24 * j, 8), 24), :]

    def stat_copy(j):
        return pltpu.make_async_remote_copy(
            src_ref=stat_rows(stat_out, j),
            dst_ref=stat_rows(stat_in, j),
            send_sem=back_send.at[j],
            recv_sem=back_recv.at[j],
            device_id=at(source(j)),
            device_id_type=MESH,
        )

    def shift_rows(g):
        def arrive(j, inner):
            @pl.when(lax.rem(j, 8) > 0)
            def _():
                row_copy(j).wait_recv()

            return inner

        lax.fori_loop(4 * g, 4 * g + 4, arrive, 0)
        slot = lax.rem(g, AHEAD)
        rows = pl.ds(pl.multiple_of(64 * g, 64), 64)
        notes = dot(
            perm_ref[0],
            jnp.concatenate([recv[rows, 6144:6272], recv[rows, 6272:6400]], axis=0),
        )
        notes_s[slot] = notes
        group_rows = flag(notes[:, 27:28] == key16)
        for c in range(2):
            for t in range(TRANS):
                at_row = c * 432 + t * 48
                oh_s[at_row : at_row + 48, :] = flag(notes[48 * c : 48 * c + 48, t : t + 1] == key64)
        for base in range(0, PIX, CHUNK):
            here = slice(base, base + CHUNK)
            extra = recv[rows, 2 * PIX + base : 2 * PIX + base + CHUNK]
            weights = dot(group_rows, wtab[:, here])
            real = jnp.concatenate([recv[rows, here], extra], axis=0)
            imag = jnp.concatenate([recv[rows, PIX + base : PIX + base + CHUNK], extra], axis=0)
            wr_s[:, here] = weights * dot(perm_ref[0], real)
            wi_s[:, here] = weights * dot(perm_ref[1], imag)
        for base in range(0, PIX, CHUNK):
            here = slice(base, base + CHUNK)
            there = slice(PIX + base, PIX + base + CHUNK)
            cosines = dot(oh_s[...], trig[:, here])
            sines = dot(oh_s[...], trig[:, there])
            for c in range(2):
                wr = wr_s[48 * c : 48 * c + 48, here]
                wi = wi_s[48 * c : 48 * c + 48, here]
                for t in range(TRANS):
                    at_row = c * 432 + t * 48
                    span = slice(at_row, at_row + 48)
                    cosine, sine = cosines[span], sines[span]
                    a_s[slot, span, here] = (wr * cosine + wi * sine).astype(jnp.bfloat16)
                    a_s[slot, span, there] = (wi * cosine - wr * sine).astype(jnp.bfloat16)

    def score(n):
        g, c = n // 2, lax.rem(n, 2)
        slot = lax.rem(g, AHEAD)
        notes = notes_s[slot, pl.ds(pl.multiple_of(48 * c, 16), 48), :]
        group_rows = flag(notes[:, 27:28] == key16[0:48])
        acc[...] = dot_nt(a_s[slot, pl.ds(pl.multiple_of(432 * c, 16), 432), :], pbuf[c])
        penalty = dot(group_rows, pentab[c])
        top = acc[0:48, :]
        for t in range(1, TRANS):
            top = jnp.maximum(top, acc[48 * t : 48 * t + 48, :])
        highest = jnp.max(top + penalty, axis=1, keepdims=True)
        offset = penalty - highest
        total = jnp.zeros((48, 256), jnp.float32)
        sum_x = jnp.zeros((48, 256), jnp.float32)
        sum_y = jnp.zeros((48, 256), jnp.float32)
        for t in range(TRANS):
            term = jnp.exp(acc[48 * t : 48 * t + 48, :] + offset)
            total = total + term
            sum_x = sum_x + term * notes[:, 9 + t : 10 + t]
            sum_y = sum_y + term * notes[:, 18 + t : 19 + t]
        total = jnp.sum(total, axis=1, keepdims=True)
        mean_x = jnp.sum(sum_x, axis=1, keepdims=True) / total
        mean_y = jnp.sum(sum_y, axis=1, keepdims=True) / total
        log_weight = highest + jnp.log(total)
        stats = jnp.where(stat_lane == 0, log_weight, jnp.where(stat_lane == 1, mean_x, mean_y))
        for half in range(2):

            @pl.when(c == half)
            def _(half=half):
                for s in range(4):
                    spot = pl.ds(96 * g + 24 * s + CAP * half, CAP)
                    stat_out[spot, :] = stats[CAP * s : CAP * s + CAP, :]

        def give_back(j, inner):
            @pl.when(j > 0)
            def _():
                stat_copy(j).start()

            return inner

        @pl.when(c == 1)
        def _():
            lax.fori_loop(4 * g, 4 * g + 4, give_back, 0)

    def prepare(_):
        wtab[...] = jnp.zeros_like(wtab)
        pentab[...] = jnp.zeros_like(pentab)
        for part, piece in enumerate(split3(ctf_ref[...] / sig_ref[...])):
            wtab[16 * part : 16 * part + 16, :] = piece
        class_lanes = lax.broadcasted_iota(jnp.int32, (128, 64), 1)
        own_notes = meta_all[0].astype(jnp.float32)
        picks = [own_notes[:, 28 + k : 29 + k].astype(jnp.int32) for k in range(2)]
        hot = [class_lanes == pick for pick in picks]
        after = flag(
            lax.broadcasted_iota(jnp.int32, (128, 128), 1)
            < lax.broadcasted_iota(jnp.int32, (128, 128), 0)
        )
        ranks = dot(after, flag(hot[0] | hot[1]))
        spots = []
        for k in range(2):
            rank = jnp.sum(jnp.where(hot[k], ranks, 0.0), axis=1, keepdims=True).astype(jnp.int32)
            owner = picks[k] // 2
            dc = lax.rem(lax.rem(owner, 2) + core, 2)
            oy, oz = lax.rem(owner // 2, 4), owner // 8
            place = oz * (1 - core) + oy * core
            cross = oy * (1 - core) + oz * core
            ahead = lax.rem(place - along + 4, 4)
            b = jnp.where(ahead == 3, 2, jnp.where(ahead == 2, 3, ahead))
            j = b * 8 + flip(cross, other) * 2 + dc
            spots.append(24 * j + CAP * lax.rem(picks[k], 2) + rank)
        stat_cols = lax.broadcasted_iota(jnp.int32, (128, 24 * PEERS), 1)
        for k in range(2):
            finder[128 * k : 128 * k + 128, :] = flag(stat_cols == spots[k])

    def turn(v, carry):
        def chosen(kind):
            spots = [at_v for at_v, op in enumerate(ORDER) if op[0] == kind]
            here, arg = v == spots[0], int(ORDER[spots[0]][1:] or 0)
            for at_v in spots[1:]:
                arg = jnp.where(v == at_v, int(ORDER[at_v][1:] or 0), arg)
                here = here | (v == at_v)
            return here, arg

        for kind, work in (
            ("P", pack),
            ("K", prepare),
            ("W", pass_on),
            ("F", forward),
            ("G", shift_rows),
            ("V", whole_views),
            ("S", score),
        ):
            here, arg = chosen(kind)

            @pl.when(here)
            def _(work=work, arg=arg):
                work(arg)

        return carry

    lax.fori_loop(0, len(ORDER), turn, 0)
    stat_in[0:24, :] = stat_out[0:24, :]

    def returned(j, inner):
        stat_copy(j).wait_recv()
        return inner

    lax.fori_loop(1, PEERS, returned, 0)
    parts = split3(stat_in[...])
    found = dot(finder[...], parts[0]) + dot(finder[...], parts[1]) + dot(finder[...], parts[2])
    logs = [found[0:128, 0:1], found[128:256, 0:1]]
    peak = jnp.maximum(logs[0], logs[1])
    raw = [jnp.exp(logs[0] - peak), jnp.exp(logs[1] - peak)]
    whole = raw[0] + raw[1]
    probs = [raw[0] / whole, raw[1] / whole]
    lane = lax.broadcasted_iota(jnp.int32, (128, 128), 1)
    mean_x = probs[0] * found[0:128, 1:2] + probs[1] * found[128:256, 1:2]
    mean_y = probs[0] * found[0:128, 2:3] + probs[1] * found[128:256, 2:3]
    result = jnp.where(
        lane < 2,
        jnp.where(lane == 0, probs[0], probs[1]),
        jnp.where(lane == 2, mean_x, mean_y),
    ).T
    out_ref[...] = result[0:4, :]

    def finish(j, inner):
        @pl.when(lax.rem(j, 8) > 0)
        def _():
            row_copy(j).wait_send()

        stat_copy(j).wait_send()
        return inner

    lax.fori_loop(1, PEERS, finish, 0)
    for lap in laps:
        lap.wait_send()
    for c in range(2):
        for copy in (own_right(c), own_left(c), on_right(c), on_left(c)):
            copy.wait_send()


def on_device(particles, candidates, ctf_ids, offsets, ctf_table, sigma_sq, projections):
    vmem = pl.BlockSpec(memory_space=pltpu.VMEM)
    hbm = pl.BlockSpec(memory_space=pl.ANY)
    out = jax.ShapeDtypeStruct((4, 128), jnp.float32)
    f32, bf16 = jnp.float32, jnp.bfloat16
    dma = pltpu.SemaphoreType.DMA
    both = pl.pallas_call(
        kernel,
        out_shape=out,
        in_specs=[hbm] + [vmem] * 6 + [hbm] * 2,
        out_specs=vmem,
        scratch_shapes=[
            pltpu.VMEM((4, 128, 2 * PIX), bf16),
            pltpu.VMEM((128, 128), f32),
            pltpu.VMEM((256, 24 * PEERS), bf16),
            pltpu.VMEM((4, 128, 128), bf16),
            pltpu.VMEM((16 * PEERS, WIDE), bf16),
            pltpu.VMEM((16 * PEERS, WIDE), bf16),
            pltpu.VMEM((2, 256, 2 * PIX), bf16),
            pltpu.VMEM((256, 2 * PIX), bf16),
            pltpu.VMEM((64, 128), f32),
            pltpu.VMEM((128, 128), bf16),
            pltpu.VMEM((128, 256), bf16),
            pltpu.VMEM((128, PIX), bf16),
            pltpu.VMEM((2, 128, 256), bf16),
            pltpu.VMEM((ROWS, 256), bf16),
            pltpu.VMEM((96, PIX), f32),
            pltpu.VMEM((96, PIX), f32),
            pltpu.VMEM((AHEAD, ROWS, 2 * PIX), bf16),
            pltpu.VMEM((AHEAD, 96, 128), f32),
            pltpu.VMEM((ROWS // 2, 256), f32),
            pltpu.VMEM((24 * PEERS, 128), f32),
            pltpu.VMEM((24 * PEERS, 128), f32),
            dma((PEERS,)),
            dma((PEERS,)),
            dma((PEERS,)),
            dma((PEERS,)),
            dma((8,)),
            dma((8,)),
            dma((9,)),
            dma((9,)),
            dma((4,)),
        ],
        compiler_params=pltpu.CompilerParams(
            collective_id=0, has_side_effects=True, vmem_limit_bytes=60 * 1024 * 1024
        ),
    )(
        particles,
        candidates.T,
        ctf_ids[None, :],
        offsets.transpose(2, 1, 0),
        ctf_table,
        sigma_sq[None, :],
        jnp.asarray(unpack_perm()),
        jnp.asarray(trig_table()),
        projections,
    )
    return both[0:2].T, both[2:4].T


def solution(mesh):
    in_specs = (
        P(("pose", "dom"), None),
        P(("pose", "dom"), None),
        P(("pose", "dom")),
        P(("pose", "dom"), None, None),
        P(),
        P(),
        P("pose", "dom", None),
    )
    out_specs = (P(("pose", "dom"), None), P(("pose", "dom"), None))
    return jax.shard_map(
        on_device, mesh=mesh, in_specs=in_specs, out_specs=out_specs, check_vma=False
    )
```

```python
import math

import jax
import jax.numpy as jnp
import numpy as np
from jax import lax
from jax.experimental import pallas as pl
from jax.experimental.pallas import tpu as pltpu
from jax.sharding import PartitionSpec as P

MESH = pl.DeviceIdType.MESH
BOX = 128
PIX = 2048
TRANS = 9
CAP = 12
PEERS = 32
CHUNK = 512
WIDE = 6400
ROWS = 864
AHEAD = 4
ORDER = "P0 K G0 W F0 G1 V0 S0 P1 S2 P2 P3 F1 G2 S4 G3 S6 V1 S1 S3 S5 S7 G4 S8 S9 G5 S10 S11 G6 S12 S13 G7 S14 S15".split()


def trig_table():
    pixel = np.arange(PIX)
    kx, ky = pixel % 64 - 32, pixel // 64
    both = np.zeros((49, 2 * PIX), np.float64)
    for ox in range(-3, 4):
        for oy in range(-3, 4):
            angle = 2.0 * math.pi * ((kx * ox + ky * oy) % BOX) / BOX
            both[(ox + 3) * 7 + oy + 3] = np.concatenate([np.cos(angle), np.sin(angle)])
    table = np.zeros((256, 2 * PIX), jnp.bfloat16)
    left = both
    for part in range(3):
        piece = left.astype(jnp.bfloat16)
        table[64 * part : 64 * part + 49] = piece
        left = left - piece.astype(np.float64)
    return table


def unpack_perm():
    perm = np.zeros((2, 96, 128), np.float32)
    for m in range(48):
        src, k = divmod(m, CAP)
        perm[:, m, src * 16 + k] = 1.0
        for part in range(2):
            col = src * 16 + 12 + k if k < 4 else 64 + src * 16 + 8 * part + k - 4
            perm[part, 48 + m, col] = 1.0
    return perm.astype(jnp.bfloat16)


def dot(a, b):
    return jnp.dot(a, b, preferred_element_type=jnp.float32)


def dot_nt(a, b):
    return lax.dot_general(a, b, (((1,), (1,)), ((), ())), preferred_element_type=jnp.float32)


def split3(value):
    first = value.astype(jnp.bfloat16)
    rest = value - first.astype(jnp.float32)
    second = rest.astype(jnp.bfloat16)
    third = (rest - second.astype(jnp.float32)).astype(jnp.bfloat16)
    return first, second, third


def flag(cond):
    return jnp.where(cond, 1.0, 0.0).astype(jnp.bfloat16)


def fiota(shape, dim):
    return lax.broadcasted_iota(jnp.int32, shape, dim).astype(jnp.float32)


def kernel(
    x_hbm,
    cand_ref,
    ids_ref,
    off_ref,
    ctf_ref,
    sig_ref,
    perm_ref,
    trig_hbm,
    proj_hbm,
    out_ref,
    x_all,
    note_s,
    finder,
    meta_all,
    send,
    recv,
    pbuf,
    trig,
    q_s,
    s1,
    s2,
    wtab,
    pentab,
    oh_s,
    wr_s,
    wi_s,
    a_s,
    notes_s,
    acc,
    stat_out,
    stat_in,
    send_sem,
    recv_sem,
    back_send,
    back_recv,
    ag_send,
    ag_recv,
    lap_send,
    lap_recv,
    local_sem,
):
    me = lax.axis_index("pose")
    dom = lax.axis_index("dom")
    core, my, mz = lax.rem(me, 2), lax.rem(me // 2, 4), me // 8
    along, other = mz * (1 - core) + my * core, my * (1 - core) + mz * core
    along_step, other_step = 8 - 6 * core, 2 + 6 * core

    def flip(a, b):
        hi = lax.rem(a // 2 + b // 2, 2)
        lo = lax.rem(lax.rem(a, 2) + lax.rem(b, 2), 2)
        return 2 * hi + lo

    def pose_of(place, cross, which):
        return place * along_step + cross * other_step + which

    def taker(i):
        return pose_of(along, flip(other, i // 2), lax.rem(core + lax.rem(i, 2), 2))

    def source(j):
        turn, a, c = j // 8, lax.rem(j // 2, 4), lax.rem(j, 2)
        reach = turn + (turn // 2) * (1 - 2 * lax.rem(turn, 2))
        place = (1 - c) * lax.rem(along - reach + 4, 4) + c * flip(along, a)
        cross = (1 - c) * flip(other, a) + c * lax.rem(other - reach + 4, 4)
        return pose_of(place, cross, lax.rem(core + c, 2))

    def at(p):
        return {"pose": p, "dom": dom}

    right = {"pose": me, "dom": lax.rem(dom + 1, 4)}
    left = {"pose": me, "dom": lax.rem(dom + 3, 4)}
    across = {"pose": me, "dom": lax.rem(dom + 2, 4)}

    barrier = pltpu.get_barrier_semaphore()

    def greet(j, carry):
        pl.semaphore_signal(
            barrier, inc=1, device_id=at(lax.rem(me + j, PEERS)), device_id_type=MESH
        )
        return carry

    lax.fori_loop(1, PEERS, greet, 0)
    for peer in (right, left, across):
        pl.semaphore_signal(barrier, inc=1, device_id=peer, device_id_type=MESH)

    own_copies = [
        pltpu.make_async_copy(proj_hbm.at[c], pbuf.at[c, pl.ds(0, 64)], local_sem.at[c])
        for c in range(2)
    ]
    own_copies.append(pltpu.make_async_copy(trig_hbm, trig, local_sem.at[2]))
    own_copies.append(pltpu.make_async_copy(x_hbm, x_all.at[0], local_sem.at[3]))
    for copy in own_copies[::-1]:
        copy.start()

    class_rows = fiota((64, 128), 0)
    before = flag(
        lax.broadcasted_iota(jnp.int32, (128, 128), 0)
        < lax.broadcasted_iota(jnp.int32, (128, 128), 1)
    )
    name_lanes = flag(
        lax.broadcasted_iota(jnp.int32, (16, 128), 1)
        == lax.broadcasted_iota(jnp.int32, (16, 128), 0) + 28
    )
    slot_rows = fiota((16, 128), 0)
    note_s[...] = jnp.zeros_like(note_s)
    for t in range(TRANS):
        shift_x = off_ref[t, 0:1, :].astype(jnp.float32)
        shift_y = off_ref[t, 1:2, :].astype(jnp.float32)
        note_s[t : t + 1, :] = (shift_x + 3.0) * 7.0 + shift_y + 3.0
        note_s[9 + t : 10 + t, :] = shift_x
        note_s[18 + t : 19 + t, :] = shift_y
    note_s[27:28, :] = ids_ref[...].astype(jnp.float32)
    note_s[28:30, :] = cand_ref[...].astype(jnp.float32)
    meta_all[0] = note_s[...].T.astype(jnp.bfloat16)

    def block(ref, j):
        return ref.at[pl.ds(pl.multiple_of(16 * j, 16), 16), :]

    def row_copy(j):
        return pltpu.make_async_remote_copy(
            src_ref=block(send, j),
            dst_ref=block(recv, j),
            send_sem=send_sem.at[j],
            recv_sem=recv_sem.at[j],
            device_id=at(taker(lax.rem(j, 8))),
            device_id_type=MESH,
        )

    up = at(pose_of(lax.rem(along + 1, 4), other, core))
    down = at(pose_of(lax.rem(along + 3, 4), other, core))

    def lap_copy(src, dst, sem, device):
        return pltpu.make_async_remote_copy(
            src_ref=src,
            dst_ref=dst,
            send_sem=lap_send.at[sem],
            recv_sem=lap_recv.at[sem],
            device_id=device,
            device_id_type=MESH,
        )

    first, second = pl.ds(0, 64), pl.ds(64, 64)
    laps = [
        lap_copy(meta_all.at[0], meta_all.at[1], 0, up),
        lap_copy(x_all.at[0, first], x_all.at[1, first], 1, up),
        lap_copy(x_all.at[0, second], x_all.at[1, second], 2, up),
        lap_copy(meta_all.at[0], meta_all.at[2], 3, down),
        lap_copy(x_all.at[0, second], x_all.at[2, second], 4, down),
        lap_copy(x_all.at[0, first], x_all.at[2, first], 5, down),
        lap_copy(meta_all.at[1], meta_all.at[3], 6, up),
        lap_copy(x_all.at[1, first], x_all.at[3, first], 7, up),
        lap_copy(x_all.at[2, second], x_all.at[3, second], 8, down),
    ]

    def view_copy(src, dst, sem, device):
        return pltpu.make_async_remote_copy(
            src_ref=src,
            dst_ref=dst,
            send_sem=ag_send.at[sem],
            recv_sem=ag_recv.at[sem],
            device_id=device,
            device_id_type=MESH,
        )

    def own_right(c):
        return view_copy(pbuf.at[c, pl.ds(0, 64)], pbuf.at[c, pl.ds(64, 64)], c, right)

    def own_left(c):
        return view_copy(pbuf.at[c, pl.ds(0, 64)], pbuf.at[c, pl.ds(192, 64)], 2 + c, left)

    def on_right(c):
        return view_copy(pbuf.at[c, pl.ds(64, 32)], pbuf.at[c, pl.ds(128, 32)], 4 + c, right)

    def on_left(c):
        return view_copy(pbuf.at[c, pl.ds(224, 32)], pbuf.at[c, pl.ds(160, 32)], 6 + c, left)

    pl.semaphore_wait(barrier, PEERS - 1 + 3)
    own_copies[3].wait()
    for k in (0, 1, 3, 4):
        laps[k].start()
    own_copies[0].wait()
    own_copies[1].wait()
    own_right(0).start()
    own_left(0).start()
    laps[2].start()
    laps[5].start()

    def pass_on(_):
        laps[0].wait_recv()
        laps[1].wait_recv()
        laps[6].start()
        laps[7].start()
        laps[4].wait_recv()
        laps[8].start()

    def pack(b):
        @pl.when(b == 1)
        def _():
            laps[2].wait_recv()

        @pl.when(b == 2)
        def _():
            laps[3].wait_recv()
            laps[5].wait_recv()

        @pl.when(b == 3)
        def _():
            for lap in laps[6:]:
                lap.wait_recv()

        notes = meta_all[b]
        names = dot_nt(name_lanes, notes)
        named = (class_rows == names[0:1, :]) | (class_rows == names[1:2, :])
        q_s[...] = jnp.where(named, dot(flag(named), before), -1.0)
        for i in range(8):
            p = taker(i)
            qa = q_s[pl.ds(2 * p, 1), :]
            qb = q_s[pl.ds(2 * p + 1, 1), :]
            rows = slice(16 * i, 16 * i + 16)
            s1[rows, :] = flag(
                jnp.where(slot_rows < 12.0, qa, qb)
                == jnp.where(slot_rows < 12.0, slot_rows, slot_rows - 12.0)
            )
            s2[rows, 0:128] = flag((qb == slot_rows + 4.0) & (slot_rows < 8.0))
            s2[rows, 128:256] = flag((qb == slot_rows - 4.0) & (slot_rows >= 8.0))
        rows = pl.ds(pl.multiple_of(128 * b, 128), 128)
        for start in range(0, 2 * PIX, CHUNK):
            send[rows, start : start + CHUNK] = dot(
                s1[...], x_all[b, :, start : start + CHUNK]
            ).astype(jnp.bfloat16)
        for start in range(0, PIX, CHUNK):
            pair = jnp.concatenate(
                [
                    x_all[b, :, start : start + CHUNK],
                    x_all[b, :, PIX + start : PIX + start + CHUNK],
                ],
                axis=0,
            )
            send[rows, 2 * PIX + start : 2 * PIX + start + CHUNK] = dot(s2[...], pair).astype(
                jnp.bfloat16
            )
        send[rows, 6144:6272] = dot(s1[...], notes).astype(jnp.bfloat16)
        send[rows, 6272:6400] = dot(s2[:, 0:128], notes).astype(jnp.bfloat16)

        def launch(i, inner):
            row_copy(8 * b + i).start()
            return inner

        lax.fori_loop(1, 8, launch, 0)
        mine = pl.ds(pl.multiple_of(128 * b, 128), 16)
        recv[mine, :] = send[mine, :]

    own_copies[2].wait()

    def forward(c):
        own_right(c).wait_recv()
        on_right(c).start()
        own_left(c).wait_recv()
        on_left(c).start()

        @pl.when(c == 0)
        def _():
            own_right(1).start()
            own_left(1).start()

    def whole_views(c):
        on_right(c).wait_recv()
        on_left(c).wait_recv()
        damping = ctf_ref[...] / sig_ref[...] * ctf_ref[...]
        penalty = jnp.zeros((16, 256), jnp.float32)
        for start in range(0, PIX, CHUNK):
            real = pbuf[c, :, start : start + CHUNK].astype(jnp.float32)
            imag = pbuf[c, :, PIX + start : PIX + start + CHUNK].astype(jnp.float32)
            penalty = penalty + lax.dot_general(
                damping[:, start : start + CHUNK],
                real * real + imag * imag,
                (((1,), (1,)), ((), ())),
                precision=lax.Precision.HIGHEST,
                preferred_element_type=jnp.float32,
            )
        for part, piece in enumerate(split3(-0.5 * penalty)):
            pentab[c, 16 * part : 16 * part + 16, :] = piece

    lanes = lax.broadcasted_iota(jnp.int32, (48, 256), 1)
    key64 = lax.rem(lanes, 64).astype(jnp.float32)
    key16 = lax.rem(lax.broadcasted_iota(jnp.int32, (96, 128), 1), 16).astype(jnp.float32)
    stat_lane = lax.broadcasted_iota(jnp.int32, (48, 128), 1)

    def stat_rows(ref, j):
        return ref.at[pl.ds(pl.multiple_of(24 * j, 8), 24), :]

    def stat_copy(j):
        return pltpu.make_async_remote_copy(
            src_ref=stat_rows(stat_out, j),
            dst_ref=stat_rows(stat_in, j),
            send_sem=back_send.at[j],
            recv_sem=back_recv.at[j],
            device_id=at(source(j)),
            device_id_type=MESH,
        )

    def shift_rows(g):
        def arrive(j, inner):
            @pl.when(lax.rem(j, 8) > 0)
            def _():
                row_copy(j).wait_recv()

            return inner

        lax.fori_loop(4 * g, 4 * g + 4, arrive, 0)
        slot = lax.rem(g, AHEAD)
        rows = pl.ds(pl.multiple_of(64 * g, 64), 64)
        notes = dot(
            perm_ref[0],
            jnp.concatenate([recv[rows, 6144:6272], recv[rows, 6272:6400]], axis=0),
        )
        notes_s[slot] = notes
        group_rows = flag(notes[:, 27:28] == key16)
        for c in range(2):
            for t in range(TRANS):
                at_row = c * 432 + t * 48
                oh_s[at_row : at_row + 48, :] = flag(notes[48 * c : 48 * c + 48, t : t + 1] == key64)
        for base in range(0, PIX, CHUNK):
            here = slice(base, base + CHUNK)
            extra = recv[rows, 2 * PIX + base : 2 * PIX + base + CHUNK]
            weights = dot(group_rows, wtab[:, here])
            real = jnp.concatenate([recv[rows, here], extra], axis=0)
            imag = jnp.concatenate([recv[rows, PIX + base : PIX + base + CHUNK], extra], axis=0)
            wr_s[:, here] = weights * dot(perm_ref[0], real)
            wi_s[:, here] = weights * dot(perm_ref[1], imag)
        for base in range(0, PIX, CHUNK):
            here = slice(base, base + CHUNK)
            there = slice(PIX + base, PIX + base + CHUNK)
            cosines = dot(oh_s[...], trig[:, here])
            sines = dot(oh_s[...], trig[:, there])
            for c in range(2):
                wr = wr_s[48 * c : 48 * c + 48, here]
                wi = wi_s[48 * c : 48 * c + 48, here]
                for t in range(TRANS):
                    at_row = c * 432 + t * 48
                    span = slice(at_row, at_row + 48)
                    cosine, sine = cosines[span], sines[span]
                    a_s[slot, span, here] = (wr * cosine + wi * sine).astype(jnp.bfloat16)
                    a_s[slot, span, there] = (wi * cosine - wr * sine).astype(jnp.bfloat16)

    def score(n):
        g, c = n // 2, lax.rem(n, 2)
        slot = lax.rem(g, AHEAD)
        notes = notes_s[slot, pl.ds(pl.multiple_of(48 * c, 16), 48), :]
        group_rows = flag(notes[:, 27:28] == key16[0:48])
        acc[...] = dot_nt(a_s[slot, pl.ds(pl.multiple_of(432 * c, 16), 432), :], pbuf[c])
        penalty = dot(group_rows, pentab[c])
        top = acc[0:48, :]
        for t in range(1, TRANS):
            top = jnp.maximum(top, acc[48 * t : 48 * t + 48, :])
        highest = jnp.max(top + penalty, axis=1, keepdims=True)
        offset = penalty - highest
        total = jnp.zeros((48, 256), jnp.float32)
        sum_x = jnp.zeros((48, 256), jnp.float32)
        sum_y = jnp.zeros((48, 256), jnp.float32)
        for t in range(TRANS):
            term = jnp.exp(acc[48 * t : 48 * t + 48, :] + offset)
            total = total + term
            sum_x = sum_x + term * notes[:, 9 + t : 10 + t]
            sum_y = sum_y + term * notes[:, 18 + t : 19 + t]
        total = jnp.sum(total, axis=1, keepdims=True)
        mean_x = jnp.sum(sum_x, axis=1, keepdims=True) / total
        mean_y = jnp.sum(sum_y, axis=1, keepdims=True) / total
        log_weight = highest + jnp.log(total)
        stats = jnp.where(stat_lane == 0, log_weight, jnp.where(stat_lane == 1, mean_x, mean_y))
        for half in range(2):

            @pl.when(c == half)
            def _(half=half):
                for s in range(4):
                    spot = pl.ds(96 * g + 24 * s + CAP * half, CAP)
                    stat_out[spot, :] = stats[CAP * s : CAP * s + CAP, :]

        def give_back(j, inner):
            @pl.when(j > 0)
            def _():
                stat_copy(j).start()

            return inner

        @pl.when(c == 1)
        def _():
            lax.fori_loop(4 * g, 4 * g + 4, give_back, 0)

    def prepare(_):
        wtab[...] = jnp.zeros_like(wtab)
        pentab[...] = jnp.zeros_like(pentab)
        for part, piece in enumerate(split3(ctf_ref[...] / sig_ref[...])):
            wtab[16 * part : 16 * part + 16, :] = piece
        class_lanes = lax.broadcasted_iota(jnp.int32, (128, 64), 1)
        own_notes = meta_all[0].astype(jnp.float32)
        picks = [own_notes[:, 28 + k : 29 + k].astype(jnp.int32) for k in range(2)]
        hot = [class_lanes == pick for pick in picks]
        after = flag(
            lax.broadcasted_iota(jnp.int32, (128, 128), 1)
            < lax.broadcasted_iota(jnp.int32, (128, 128), 0)
        )
        ranks = dot(after, flag(hot[0] | hot[1]))
        spots = []
        for k in range(2):
            rank = jnp.sum(jnp.where(hot[k], ranks, 0.0), axis=1, keepdims=True).astype(jnp.int32)
            owner = picks[k] // 2
            dc = lax.rem(lax.rem(owner, 2) + core, 2)
            oy, oz = lax.rem(owner // 2, 4), owner // 8
            place = oz * (1 - core) + oy * core
            cross = oy * (1 - core) + oz * core
            ahead = lax.rem(place - along + 4, 4)
            b = jnp.where(ahead == 3, 2, jnp.where(ahead == 2, 3, ahead))
            j = b * 8 + flip(cross, other) * 2 + dc
            spots.append(24 * j + CAP * lax.rem(picks[k], 2) + rank)
        stat_cols = lax.broadcasted_iota(jnp.int32, (128, 24 * PEERS), 1)
        for k in range(2):
            finder[128 * k : 128 * k + 128, :] = flag(stat_cols == spots[k])

    def turn(v, carry):
        def chosen(kind):
            spots = [at_v for at_v, op in enumerate(ORDER) if op[0] == kind]
            here, arg = v == spots[0], int(ORDER[spots[0]][1:] or 0)
            for at_v in spots[1:]:
                arg = jnp.where(v == at_v, int(ORDER[at_v][1:] or 0), arg)
                here = here | (v == at_v)
            return here, arg

        for kind, work in (
            ("P", pack),
            ("K", prepare),
            ("W", pass_on),
            ("F", forward),
            ("G", shift_rows),
            ("V", whole_views),
            ("S", score),
        ):
            here, arg = chosen(kind)

            @pl.when(here)
            def _(work=work, arg=arg):
                work(arg)

        return carry

    lax.fori_loop(0, len(ORDER), turn, 0)
    stat_in[0:24, :] = stat_out[0:24, :]

    def returned(j, inner):
        stat_copy(j).wait_recv()
        return inner

    lax.fori_loop(1, PEERS, returned, 0)
    parts = split3(stat_in[...])
    found = dot(finder[...], parts[0]) + dot(finder[...], parts[1]) + dot(finder[...], parts[2])
    logs = [found[0:128, 0:1], found[128:256, 0:1]]
    peak = jnp.maximum(logs[0], logs[1])
    raw = [jnp.exp(logs[0] - peak), jnp.exp(logs[1] - peak)]
    whole = raw[0] + raw[1]
    probs = [raw[0] / whole, raw[1] / whole]
    lane = lax.broadcasted_iota(jnp.int32, (128, 128), 1)
    mean_x = probs[0] * found[0:128, 1:2] + probs[1] * found[128:256, 1:2]
    mean_y = probs[0] * found[0:128, 2:3] + probs[1] * found[128:256, 2:3]
    result = jnp.where(
        lane < 2,
        jnp.where(lane == 0, probs[0], probs[1]),
        jnp.where(lane == 2, mean_x, mean_y),
    ).T
    out_ref[...] = result[0:4, :]

    def finish(j, inner):
        @pl.when(lax.rem(j, 8) > 0)
        def _():
            row_copy(j).wait_send()

        stat_copy(j).wait_send()
        return inner

    lax.fori_loop(1, PEERS, finish, 0)
    for lap in laps:
        lap.wait_send()
    for c in range(2):
        for copy in (own_right(c), own_left(c), on_right(c), on_left(c)):
            copy.wait_send()


def on_device(particles, candidates, ctf_ids, offsets, ctf_table, sigma_sq, projections):
    vmem = pl.BlockSpec(memory_space=pltpu.VMEM)
    hbm = pl.BlockSpec(memory_space=pl.ANY)
    out = jax.ShapeDtypeStruct((4, 128), jnp.float32)
    f32, bf16 = jnp.float32, jnp.bfloat16
    dma = pltpu.SemaphoreType.DMA
    both = pl.pallas_call(
        kernel,
        out_shape=out,
        in_specs=[hbm] + [vmem] * 6 + [hbm] * 2,
        out_specs=vmem,
        scratch_shapes=[
            pltpu.VMEM((4, 128, 2 * PIX), bf16),
            pltpu.VMEM((128, 128), f32),
            pltpu.VMEM((256, 24 * PEERS), bf16),
            pltpu.VMEM((4, 128, 128), bf16),
            pltpu.VMEM((16 * PEERS, WIDE), bf16),
            pltpu.VMEM((16 * PEERS, WIDE), bf16),
            pltpu.VMEM((2, 256, 2 * PIX), bf16),
            pltpu.VMEM((256, 2 * PIX), bf16),
            pltpu.VMEM((64, 128), f32),
            pltpu.VMEM((128, 128), bf16),
            pltpu.VMEM((128, 256), bf16),
            pltpu.VMEM((128, PIX), bf16),
            pltpu.VMEM((2, 128, 256), bf16),
            pltpu.VMEM((ROWS, 256), bf16),
            pltpu.VMEM((96, PIX), f32),
            pltpu.VMEM((96, PIX), f32),
            pltpu.VMEM((AHEAD, ROWS, 2 * PIX), bf16),
            pltpu.VMEM((AHEAD, 96, 128), f32),
            pltpu.VMEM((ROWS // 2, 256), f32),
            pltpu.VMEM((24 * PEERS, 128), f32),
            pltpu.VMEM((24 * PEERS, 128), f32),
            dma((PEERS,)),
            dma((PEERS,)),
            dma((PEERS,)),
            dma((PEERS,)),
            dma((8,)),
            dma((8,)),
            dma((9,)),
            dma((9,)),
            dma((4,)),
        ],
        compiler_params=pltpu.CompilerParams(
            collective_id=0, has_side_effects=True, vmem_limit_bytes=60 * 1024 * 1024
        ),
    )(
        particles,
        candidates.T,
        ctf_ids[None, :],
        offsets.transpose(2, 1, 0),
        ctf_table,
        sigma_sq[None, :],
        jnp.asarray(unpack_perm()),
        jnp.asarray(trig_table()),
        projections,
    )
    return both[0:2].T, both[2:4].T


def solution(mesh):
    in_specs = (
        P(("pose", "dom"), None),
        P(("pose", "dom"), None),
        P(("pose", "dom")),
        P(("pose", "dom"), None, None),
        P(),
        P(),
        P("pose", "dom", None),
    )
    out_specs = (P(("pose", "dom"), None), P(("pose", "dom"), None))
    return jax.shard_map(
        on_device, mesh=mesh, in_specs=in_specs, out_specs=out_specs, check_vma=False
    )
```
